512 devices in a mesh: seq: 16 (over z_lo, x), mp: 32 (over y, z_hi, core).
Axes of the slice: x: 4, y: 8, z: 8 (z_hi: 2, z_lo: 4; z = z_hi * 4 + z_lo), core: 2. Of those that a mesh axis runs over, the one named last changes fastest.
Arguments:
- queries: bfloat16 [65536, 1024], P(('seq', 'mp')), may hold values from -6 to 6
- keys: bfloat16 [65536, 1024], P(('seq', 'mp')), may hold values from -6 to 6
- values: bfloat16 [65536, 1024], P(('seq', 'mp')), may hold values from -6 to 6
- out_weight: bfloat16 [1024, 1024], P('mp'), may hold values from -0.1875 to 0.1875
- upstream: bfloat16 [65536, 1024], P(('seq', 'mp')), may hold values from -6 to 6
- adjacency: int32 [512, 4], P(('seq', 'mp')), may hold values 0 or 1
- counts: int32 [512], P(('seq', 'mp')), may hold values from 32 to 128, as said below
Outputs:
- mixed_out: bfloat16 [65536, 1024], P(('seq', 'mp'))
- grad_queries: bfloat16 [65536, 1024], P(('seq', 'mp'))
- grad_keys: bfloat16 [65536, 1024], P(('seq', 'mp'))
- grad_values: bfloat16 [65536, 1024], P(('seq', 'mp'))
The draws below stay inside these ranges and needn't reach their ends.
Inputs may be any that keep to these rules, and one draw needn't show every extreme that they name: `counts`: each block has between 32 and 128 valid slots; some block has exactly 128 and some exactly 32.
All inputs are finite; a program needn't handle non-finite values. No bound on the sum of `adjacency` on one device may be relied on, other than what follows from the above.
Results may differ from the reference program's by a relative error of at most 0.023.
Values may be sent and summed in bfloat16 or wider, within the bound.
A program may use at most 64 MiB of HBM per device.

```python
import jax
import jax.numpy as jnp
from jax import lax

D = 1024
HEADS = 16
HEAD_DIM = 64
TOK_DEV = 128
CYCLE = 16
COLUMNS = 32
BLOCKS = 512
TOKENS = 65536


def drawn_pair(key):
    query_key = jax.random.fold_in(key, 11)
    key_key = jax.random.fold_in(key, 12)
    out_queries = jnp.clip(jax.random.normal(query_key, (TOKENS, D), jnp.float32), -6.0, 6.0)
    out_keys = jnp.clip(jax.random.normal(key_key, (TOKENS, D), jnp.float32), -6.0, 6.0)
    return (out_queries, out_keys)


def draw_queries(key, part):
    return drawn_pair(key)[0].astype(jnp.bfloat16)


def draw_keys(key, part):
    return drawn_pair(key)[1].astype(jnp.bfloat16)


def draw_counts(key, part):
    count_key = jax.random.fold_in(key, 21)
    full_key = jax.random.fold_in(key, 22)
    step_key = jax.random.fold_in(key, 23)
    drawn = jax.random.randint(count_key, (BLOCKS,), TOK_DEV // 4, TOK_DEV + 1)
    full_index = jax.random.randint(full_key, (), 0, BLOCKS)
    least_index = (full_index + 1 + jax.random.randint(step_key, (), 0, BLOCKS - 1)) % BLOCKS
    block_ids = jnp.arange(BLOCKS, dtype=jnp.int32)
    drawn = jnp.where(block_ids == full_index, TOK_DEV, drawn)
    drawn = jnp.where(block_ids == least_index, TOK_DEV // 4, drawn)
    return drawn.astype(jnp.int32)


def plant(values, own_key, smallest, largest):
    place = [jax.random.randint(jax.random.fold_in(own_key, axis), (), 0, length) for axis, length in enumerate(values.shape)]
    widest = values.shape.index(max(values.shape))
    next_to = place[:widest] + [(place[widest] + 1) % values.shape[widest]] + place[widest + 1:]
    return values.at[tuple(place)].set(smallest).at[tuple(next_to)].set(largest)


def block_scale(stream_key, shape, split, least, largest):
    gain = 1.0
    for axis_at, blocks in split:
        heights = jax.random.uniform(jax.random.fold_in(jax.random.fold_in(stream_key, 6), axis_at), (blocks,), jnp.float32, least / len(split), largest / len(split))
        gain = gain * jnp.repeat(jnp.exp(heights), shape[axis_at] // blocks).reshape((-1,) + (1,) * (len(shape) - 1 - axis_at))
    return gain


def gaussian(key, shape, spread, reach, pieces=(), kind=jnp.bfloat16):
    loudness = block_scale(key, shape, pieces, -0.22, 0.18) if pieces else 1.0
    values = jax.random.normal(key, shape, jnp.float32) * spread * loudness
    return jnp.minimum(jnp.maximum(values, -reach), reach).astype(kind)


def setup_inputs(seed: int = 0) -> dict:
    key_of = jax.random.split(jax.random.key(seed), 8)
    queries = draw_queries(jax.random.fold_in(key_of[7], 71), 0)
    keys = draw_keys(jax.random.fold_in(key_of[7], 71), 0)
    values = gaussian(key_of[2], (TOKENS, D), 1.0, 6.0, ((0, 512),))
    out_weight = gaussian(key_of[3], (D, D), D ** -0.5, 0.1875, ((0, 32),))
    upstream = gaussian(key_of[4], (TOKENS, D), 1.0, 6.0, ((0, 512),))
    adjacency = plant((jax.random.randint(key_of[5], (BLOCKS, 4), 0, 3) < 1).astype(jnp.int32), jax.random.fold_in(key_of[5], 1), 0, 1)
    counts = draw_counts(jax.random.fold_in(key_of[7], 71), 0)
    return {"queries": queries, "keys": keys, "values": values, "out_weight": out_weight, "upstream": upstream, "adjacency": adjacency, "counts": counts}


score_scale = 0.125
cycle_offsets = (1, -1, 2, -2)


def to_heads(matrix):
    return matrix.reshape(matrix.shape[:-1] + (HEADS, HEAD_DIM)).astype(jnp.float32)


def rounded(values_in):
    return lax.optimization_barrier(values_in.astype(jnp.bfloat16)).astype(jnp.float32)


def reference(queries, keys, values, out_weight, upstream, adjacency, counts):
    query_blocks = queries.reshape(BLOCKS, TOK_DEV, D)
    key_blocks = keys.reshape(BLOCKS, TOK_DEV, D)
    value_blocks = values.reshape(BLOCKS, TOK_DEV, D)
    offsets = jnp.array(cycle_offsets, dtype=jnp.int32)
    positions = jnp.arange(TOK_DEV, dtype=jnp.int32)

    def key_list(block_index):
        cycle_pos = block_index // COLUMNS
        lane_index = block_index % COLUMNS
        others = ((cycle_pos - offsets) % CYCLE) * COLUMNS + lane_index
        entries = jnp.concatenate([block_index[None], others]).astype(jnp.int32)
        present = jnp.concatenate([jnp.ones((1,), jnp.int32), adjacency[block_index]]) > 0
        return entries, present

    def list_scores(query_heads, key_set, count_set, present):
        scores = jnp.einsum("qhd,jkhd->jhqk", query_heads, to_heads(key_set)) * score_scale
        valid = (positions[None, :] < count_set[:, None]) & present[:, None]
        return jnp.where(valid[:, None, None, :], scores, -jnp.inf)

    def forward_block(block_index):
        entries, present = key_list(block_index)
        query_heads = to_heads(query_blocks[block_index])
        scores = list_scores(query_heads, key_blocks[entries], counts[entries], present)
        maxima = jnp.max(scores, axis=(0, 3))
        expo = jnp.exp(scores - maxima[None, :, :, None])
        totals = jnp.sum(expo, axis=(0, 3))
        probs = rounded(expo / totals[None, :, :, None])
        attended = jnp.einsum("jhqk,jkhd->qhd", probs, to_heads(value_blocks[entries]))
        return attended.reshape(TOK_DEV, D).astype(jnp.bfloat16), maxima, totals

    block_ids = jnp.arange(BLOCKS, dtype=jnp.int32)
    attended_blocks, maxima_all, totals_all = lax.map(forward_block, block_ids)
    attended = attended_blocks.reshape(TOKENS, D)
    mixed_out = jnp.dot(attended, out_weight, preferred_element_type=jnp.float32).astype(jnp.bfloat16)
    grad_attended = jnp.dot(upstream, out_weight.T, preferred_element_type=jnp.float32).astype(jnp.bfloat16)
    grad_blocks = grad_attended.reshape(BLOCKS, TOK_DEV, D)
    delta_all = jnp.einsum("bqhd,bqhd->bhq", to_heads(grad_blocks), to_heads(attended_blocks))

    def query_block_grads(block_index):
        entries, present = key_list(block_index)
        query_heads = to_heads(query_blocks[block_index])
        grad_heads = to_heads(grad_blocks[block_index])
        scores = list_scores(query_heads, key_blocks[entries], counts[entries], present)
        probs = jnp.exp(scores - maxima_all[block_index][None, :, :, None]) / totals_all[block_index][None, :, :, None]
        grad_probs = jnp.einsum("qhd,jkhd->jhqk", grad_heads, to_heads(value_blocks[entries]))
        grad_scores = rounded(probs * (grad_probs - delta_all[block_index][None, :, :, None]))
        query_term = score_scale * jnp.einsum("jhqk,jkhd->qhd", grad_scores, to_heads(key_blocks[entries]))
        return query_term.reshape(TOK_DEV, D).astype(jnp.bfloat16)

    def key_block_grads(block_index):
        cycle_pos = block_index // COLUMNS
        lane_index = block_index % COLUMNS
        sources = ((cycle_pos + offsets) % CYCLE) * COLUMNS + lane_index
        entries = jnp.concatenate([block_index[None], sources]).astype(jnp.int32)
        flags = adjacency[sources, jnp.arange(4, dtype=jnp.int32)] > 0
        present = jnp.concatenate([jnp.ones((1,), dtype=bool), flags])
        query_heads = to_heads(query_blocks[entries])
        grad_heads = to_heads(grad_blocks[entries])
        key_heads = to_heads(key_blocks[block_index])
        value_heads = to_heads(value_blocks[block_index])
        scores = jnp.einsum("jqhd,khd->jhqk", query_heads, key_heads) * score_scale
        valid = (positions < counts[block_index])[None, :] & present[:, None]
        scores = jnp.where(valid[:, None, None, :], scores, -jnp.inf)
        probs = jnp.exp(scores - maxima_all[entries][..., None]) / totals_all[entries][..., None]
        grad_probs = jnp.einsum("jqhd,khd->jhqk", grad_heads, value_heads)
        grad_scores = rounded(probs * (grad_probs - delta_all[entries][..., None]))
        key_terms = score_scale * jnp.einsum("jhqk,jqhd->jkhd", grad_scores, query_heads)
        value_terms = jnp.einsum("jhqk,jqhd->jkhd", rounded(probs), grad_heads)

        def settle(terms):
            terms = terms.reshape(5, TOK_DEV, D)
            return (terms[0] + jnp.sum(rounded(terms[1:]), axis=0)).astype(jnp.bfloat16)

        return settle(key_terms), settle(value_terms)

    grad_queries = lax.map(query_block_grads, block_ids).reshape(TOKENS, D)
    grad_keys, grad_values = lax.map(key_block_grads, block_ids)
    return mixed_out, grad_queries, grad_keys.reshape(TOKENS, D), grad_values.reshape(TOKENS, D)
```

```python
import jax
import jax.numpy as jnp
from jax import lax
from jax.experimental import pallas as pl
from jax.experimental.pallas import tpu as pltpu
from jax.sharding import PartitionSpec as P

GROUPS = 4
PAIR = 128
HALF = 64
SEQ = 16
SHARDS = 32
RING = 8
MASKED = -1e30
MESH = pl.DeviceIdType.MESH
CONTRACT_LAST = (((1,), (1,)), ((), ()))
CONTRACT_FIRST = (((0,), (0,)), ((), ()))


def dot(left, right, dims):
    return lax.dot_general(left, right, dims, preferred_element_type=jnp.float32)


def kernel(
    q_ref, k_ref, v_ref, w_ref, u_ref, cnt_ref, adj_ref,
    mix_ref, dq_ref, dk_ref, dv_ref,
    wfull, kvr, cr, tsn, trc, near, own, att, grad,
    w_send, w_recv, kv_send, kv_recv, c_send, c_recv, t_send, t_recv,
):
    seq = lax.axis_index("seq")
    mp = lax.axis_index("mp")
    rows, width = q_ref.shape
    group_width = width // GROUPS
    up = lax.rem(seq + 1, SEQ)
    down = lax.rem(seq + SEQ - 1, SEQ)
    y = mp // 4
    z_hi = lax.rem(mp // 2, 2)
    core = lax.rem(mp, 2)

    def slot_of(y_at, z_at, core_at):
        return y_at * 4 + z_at * 2 + core_at

    y_up = slot_of(lax.rem(y + 1, RING), z_hi, core)
    y_down = slot_of(lax.rem(y + RING - 1, RING), z_hi, core)
    z_other = slot_of(y, 1 - z_hi, core)
    core_other = slot_of(y, z_hi, 1 - core)

    barrier = pltpu.get_barrier_semaphore()
    for target in (up, down):
        pl.semaphore_signal(barrier, inc=1, device_id=(target, mp), device_id_type=MESH)
    for target in (y_up, y_down, z_other, core_other):
        pl.semaphore_signal(barrier, inc=1, device_id=(seq, target), device_id_type=MESH)
    pl.semaphore_wait(barrier, 6)

    w_copies = []

    def send_weight(slot, target, source):
        copy = pltpu.make_async_remote_copy(
            src_ref=source,
            dst_ref=wfull.at[slot],
            send_sem=w_send.at[len(w_copies)],
            recv_sem=w_recv.at[slot],
            device_id=(seq, target),
            device_id_type=MESH,
        )
        copy.start()
        w_copies.append(copy)

    def await_weight(slot):
        pltpu.make_async_remote_copy(
            src_ref=w_ref,
            dst_ref=wfull.at[slot],
            send_sem=w_send.at[0],
            recv_sem=w_recv.at[slot],
            device_id=(seq, core_other),
            device_id_type=MESH,
        ).wait_recv()

    def kv_copy(j, g, i):
        if j < 2:
            source = (k_ref, v_ref)[i].at[:, pl.ds(g * group_width, group_width)]
        else:
            source = kvr.at[j - 2, g, i]
        return pltpu.make_async_remote_copy(
            src_ref=source,
            dst_ref=kvr.at[j, g, i],
            send_sem=kv_send.at[j, g, i],
            recv_sem=kv_recv.at[j, g, i],
            device_id=((up, down)[j % 2], mp),
            device_id_type=MESH,
        )

    def count_copy(j):
        return pltpu.make_async_remote_copy(
            src_ref=cnt_ref if j < 2 else cr.at[j - 2],
            dst_ref=cr.at[j],
            send_sem=c_send.at[j],
            recv_sem=c_recv.at[j],
            device_id=((up, down)[j % 2], mp),
            device_id_type=MESH,
        )

    def term_copy(j, g, i):
        return pltpu.make_async_remote_copy(
            src_ref=tsn.at[j, g, i],
            dst_ref=trc.at[j, g, i],
            send_sem=t_send.at[j, g, i],
            recv_sem=t_recv.at[j, g, i],
            device_id=((down, up)[j % 2], mp),
            device_id_type=MESH,
        )

    send_weight(mp, z_other, w_ref)
    send_weight(mp, y_up, w_ref)
    send_weight(mp, y_down, w_ref)
    send_weight(mp, core_other, w_ref)
    for j in (0, 1):
        count_copy(j).start()
    for g in range(GROUPS):
        for i in (0, 1):
            for j in (0, 1):
                kv_copy(j, g, i).start()
    wfull[mp] = w_ref[...]

    await_weight(z_other)
    send_weight(z_other, y_up, wfull.at[z_other])
    send_weight(z_other, y_down, wfull.at[z_other])
    send_weight(z_other, core_other, wfull.at[z_other])
    for step in range(1, 5):
        for z_at in (z_hi, 1 - z_hi):
            slot = slot_of(lax.rem(y + RING - step, RING), z_at, core)
            await_weight(slot)
            if step < 4:
                send_weight(slot, y_up, wfull.at[slot])
            send_weight(slot, core_other, wfull.at[slot])
            if step < 4:
                slot = slot_of(lax.rem(y + step, RING), z_at, core)
                await_weight(slot)
                if step < 3:
                    send_weight(slot, y_down, wfull.at[slot])
                send_weight(slot, core_other, wfull.at[slot])

    for j in (0, 1):
        count_copy(j).wait_recv()
        count_copy(j + 2).start()
    for g in range(GROUPS):
        for i in (0, 1):
            for j in (0, 1):
                kv_copy(j, g, i).wait_recv()
                kv_copy(j + 2, g, i).start()

    for y_at in range(RING):
        for z_at in (0, 1):
            await_weight(slot_of(y_at, z_at, 1 - core))

    def weight_rows(g):
        per = SHARDS // GROUPS
        return wfull[g * per:(g + 1) * per].reshape(group_width, width)

    for g in range(GROUPS):
        grad[g] = dot(u_ref[...], weight_rows(g), CONTRACT_LAST).astype(jnp.bfloat16)

    for j in (2, 3):
        count_copy(j).wait_recv()

    positions = lax.broadcasted_iota(jnp.int32, (rows, 2 * rows), 0)
    first_half = lax.broadcasted_iota(jnp.int32, (rows, PAIR), 1) < HALF

    def stacked(pair):
        nothing = jnp.zeros_like(pair)
        return jnp.concatenate(
            [jnp.where(first_half, pair, nothing), jnp.where(first_half, nothing, pair)], axis=0
        )

    def heads_of(both):
        return jnp.concatenate([both[:HALF, :rows], both[HALF:, rows:]], axis=0)

    def part(value, e):
        return value[e * rows:(e + 1) * rows]

    def compute_pair(g, pp):
        columns = slice(pp * PAIR, (pp + 1) * PAIR)
        full = slice(g * group_width + pp * PAIR, g * group_width + (pp + 1) * PAIR)
        limits = [cnt_ref[0:1, :]]
        for j in range(4):
            limits.append(jnp.where(adj_ref[0, j] > 0, cr[j, 0:1, :], 0))
        queries = stacked(q_ref[:, full] * jnp.bfloat16(0.125))
        grad_pair = grad[g, :, columns]
        grads = stacked(grad_pair)
        keys = jnp.concatenate([k_ref[:, full]] + [kvr[j, g, 0, :, columns] for j in range(4)], axis=0)
        values = jnp.concatenate([v_ref[:, full]] + [kvr[j, g, 1, :, columns] for j in range(4)], axis=0)
        scores = dot(keys, queries, CONTRACT_LAST)
        masked = [jnp.where(positions < limits[e], part(scores, e), MASKED) for e in range(5)]
        largest = masked[0]
        for e in range(1, 5):
            largest = jnp.maximum(largest, masked[e])
        maxima = jnp.max(largest, axis=0, keepdims=True)
        expo = [jnp.exp(m - maxima) for m in masked]
        total = expo[0]
        for e in range(1, 5):
            total = total + expo[e]
        inverse = 1.0 / jnp.sum(total, axis=0, keepdims=True)
        probs = jnp.concatenate([m * inverse for m in expo], axis=0)
        rounded = probs.astype(jnp.bfloat16)
        attended = heads_of(dot(values, rounded, CONTRACT_FIRST)).astype(jnp.bfloat16).astype(jnp.float32)
        att[:, full] = attended.T.astype(jnp.bfloat16)
        product = attended * grad_pair.astype(jnp.float32).T
        delta = jnp.concatenate(
            [
                jnp.sum(product[:HALF], axis=0, keepdims=True),
                jnp.sum(product[HALF:], axis=0, keepdims=True),
            ],
            axis=1,
        )
        grad_scores = (probs * (dot(values, grads, CONTRACT_LAST) - delta)).astype(jnp.bfloat16)
        query_grad = heads_of(dot(keys, grad_scores, CONTRACT_FIRST)) * 0.125
        dq_ref[:, full] = query_grad.T.astype(jnp.bfloat16)
        key_terms = jnp.dot(grad_scores, queries, preferred_element_type=jnp.float32)
        value_terms = jnp.dot(rounded, grads, preferred_element_type=jnp.float32)
        for i, terms in ((0, key_terms), (1, value_terms)):
            own[g, i, :, columns] = part(terms, 0)
            for j in (0, 1):
                near[j, g, i, :, columns] = part(terms, j + 1)
                tsn[j + 2, g, i, :, columns] = part(terms, j + 3).astype(jnp.bfloat16)

    for g in range(GROUPS):
        for i in (0, 1):
            for j in (2, 3):
                kv_copy(j, g, i).wait_recv()
        for pp in range(group_width // PAIR):
            compute_pair(g, pp)
        for i in (0, 1):
            for j in (2, 3):
                term_copy(j, g, i).start()

    for g in range(GROUPS):
        for i in (0, 1):
            for j in (0, 1):
                term_copy(j + 2, g, i).wait_recv()
                tsn[j, g, i] = (near[j, g, i] + trc[j + 2, g, i].astype(jnp.float32)).astype(jnp.bfloat16)
                term_copy(j, g, i).start()

    whole = wfull[...].reshape(width, width)
    mix_ref[...] = jnp.dot(att[...], whole, preferred_element_type=jnp.float32).astype(jnp.bfloat16)

    for g in range(GROUPS):
        for i in (0, 1):
            total = own[g, i]
            for j in (0, 1):
                term_copy(j, g, i).wait_recv()
                total = total + trc[j, g, i].astype(jnp.float32)
            (dk_ref, dv_ref)[i][:, g * group_width:(g + 1) * group_width] = total.astype(jnp.bfloat16)

    for copy in w_copies:
        copy.wait_send()
    for j in range(4):
        count_copy(j).wait_send()
        for g in range(GROUPS):
            for i in (0, 1):
                kv_copy(j, g, i).wait_send()
                term_copy(j, g, i).wait_send()


def local(queries, keys, values, out_weight, upstream, adjacency, counts):
    rows, width = queries.shape
    group_width = width // GROUPS
    count_rows = jnp.broadcast_to(counts[:, None], (8, 2 * rows))
    vmem = pl.BlockSpec(memory_space=pltpu.VMEM)
    block = jax.ShapeDtypeStruct((rows, width), jnp.bfloat16)
    dma = pltpu.SemaphoreType.DMA
    pieces = (4, GROUPS, 2, rows, group_width)
    return pl.pallas_call(
        kernel,
        name="blocks",
        out_shape=(block, block, block, block),
        in_specs=[vmem] * 6 + [pl.BlockSpec(memory_space=pltpu.SMEM)],
        out_specs=(vmem, vmem, vmem, vmem),
        scratch_shapes=[
            pltpu.VMEM((SHARDS, width // SHARDS, width), jnp.bfloat16),
            pltpu.VMEM(pieces, jnp.bfloat16),
            pltpu.VMEM((4, 8, 2 * rows), jnp.int32),
            pltpu.VMEM(pieces, jnp.bfloat16),
            pltpu.VMEM(pieces, jnp.bfloat16),
            pltpu.VMEM((2,) + pieces[1:], jnp.float32),
            pltpu.VMEM(pieces[1:], jnp.float32),
            pltpu.VMEM((rows, width), jnp.bfloat16),
            pltpu.VMEM((GROUPS, rows, group_width), jnp.bfloat16),
            dma((32,)),
            dma((SHARDS,)),
            dma((4, GROUPS, 2)),
            dma((4, GROUPS, 2)),
            dma((4,)),
            dma((4,)),
            dma((4, GROUPS, 2)),
            dma((4, GROUPS, 2)),
        ],
        compiler_params=pltpu.CompilerParams(
            collective_id=0, has_side_effects=True, vmem_limit_bytes=50 * 1024 * 1024
        ),
    )(queries, keys, values, out_weight, upstream, count_rows, adjacency)


def solution(mesh):
    both = P(("seq", "mp"), None)
    return jax.shard_map(
        local,
        mesh=mesh,
        in_specs=(both, both, both, P("mp", None), both, both, P(("seq", "mp"))),
        out_specs=(both, both, both, both),
        check_vma=False,
    )
```

```python
import jax
import jax.numpy as jnp
from jax import lax
from jax.experimental import pallas as pl
from jax.experimental.pallas import tpu as pltpu
from jax.sharding import PartitionSpec as P

GROUPS = 4
PAIR = 128
HALF = 64
SEQ = 16
SHARDS = 32
RING = 8
MASKED = -1e30
MESH = pl.DeviceIdType.MESH
CONTRACT_LAST = (((1,), (1,)), ((), ()))
CONTRACT_FIRST = (((0,), (0,)), ((), ()))


def dot(left, right, dims):
    return lax.dot_general(left, right, dims, preferred_element_type=jnp.float32)


def kernel(
    q_hbm, k_hbm, v_hbm, w_hbm, u_hbm, cnt_ref, adj_ref,
    mix_ref, dq_ref, dk_ref, dv_ref,
    q_ref, k_ref, v_ref, w_ref, u_ref, in_sem, wfull, kvr, cr, tsn, trc, near, own, att, grad,
    w_send, w_recv, kv_send, kv_recv, c_send, c_recv, t_send, t_recv,
):
    seq = lax.axis_index("seq")
    mp = lax.axis_index("mp")
    rows, width = q_ref.shape
    group_width = width // GROUPS

    fetches = [
        pltpu.make_async_copy(source, target, in_sem.at[at])
        for at, (source, target) in enumerate(
            ((w_hbm, w_ref), (k_hbm, k_ref), (v_hbm, v_ref), (q_hbm, q_ref), (u_hbm, u_ref))
        )
    ]
    for fetch in fetches:
        fetch.start()
    up = lax.rem(seq + 1, SEQ)
    down = lax.rem(seq + SEQ - 1, SEQ)
    y = mp // 4
    z_hi = lax.rem(mp // 2, 2)
    core = lax.rem(mp, 2)

    def slot_of(y_at, z_at, core_at):
        return y_at * 4 + z_at * 2 + core_at

    y_up = slot_of(lax.rem(y + 1, RING), z_hi, core)
    y_down = slot_of(lax.rem(y + RING - 1, RING), z_hi, core)
    z_other = slot_of(y, 1 - z_hi, core)
    core_other = slot_of(y, z_hi, 1 - core)

    barrier = pltpu.get_barrier_semaphore()
    for target in (up, down):
        pl.semaphore_signal(barrier, inc=1, device_id=(target, mp), device_id_type=MESH)
    for target in (y_up, y_down, z_other, core_other):
        pl.semaphore_signal(barrier, inc=1, device_id=(seq, target), device_id_type=MESH)
    pl.semaphore_wait(barrier, 6)

    w_copies = []

    def send_weight(slot, target, source):
        copy = pltpu.make_async_remote_copy(
            src_ref=source,
            dst_ref=wfull.at[slot],
            send_sem=w_send.at[len(w_copies)],
            recv_sem=w_recv.at[slot],
            device_id=(seq, target),
            device_id_type=MESH,
        )
        copy.start()
        w_copies.append(copy)

    def await_weight(slot):
        pltpu.make_async_remote_copy(
            src_ref=w_ref,
            dst_ref=wfull.at[slot],
            send_sem=w_send.at[0],
            recv_sem=w_recv.at[slot],
            device_id=(seq, core_other),
            device_id_type=MESH,
        ).wait_recv()

    def kv_copy(j, g, i):
        if j < 2:
            source = (k_ref, v_ref)[i].at[:, pl.ds(g * group_width, group_width)]
        else:
            source = kvr.at[j - 2, g, i]
        return pltpu.make_async_remote_copy(
            src_ref=source,
            dst_ref=kvr.at[j, g, i],
            send_sem=kv_send.at[j, g, i],
            recv_sem=kv_recv.at[j, g, i],
            device_id=((up, down)[j % 2], mp),
            device_id_type=MESH,
        )

    def count_copy(j):
        return pltpu.make_async_remote_copy(
            src_ref=cnt_ref if j < 2 else cr.at[j - 2],
            dst_ref=cr.at[j],
            send_sem=c_send.at[j],
            recv_sem=c_recv.at[j],
            device_id=((up, down)[j % 2], mp),
            device_id_type=MESH,
        )

    def term_copy(j, g, i):
        return pltpu.make_async_remote_copy(
            src_ref=tsn.at[j, g, i],
            dst_ref=trc.at[j, g, i],
            send_sem=t_send.at[j, g, i],
            recv_sem=t_recv.at[j, g, i],
            device_id=((down, up)[j % 2], mp),
            device_id_type=MESH,
        )

    def relay_kv(g):
        for i in (0, 1):
            for j in (0, 1):
                kv_copy(j, g, i).wait_recv()
                kv_copy(j + 2, g, i).start()

    def ring_step(step, z_at):
        slot = slot_of(lax.rem(y + RING - step, RING), z_at, core)
        await_weight(slot)
        if step < 4:
            send_weight(slot, y_up, wfull.at[slot])
        send_weight(slot, core_other, wfull.at[slot])
        if step < 4:
            slot = slot_of(lax.rem(y + step, RING), z_at, core)
            await_weight(slot)
            if step < 3:
                send_weight(slot, y_down, wfull.at[slot])
            send_weight(slot, core_other, wfull.at[slot])

    fetches[0].wait()
    send_weight(mp, z_other, w_ref)
    send_weight(mp, y_up, w_ref)
    send_weight(mp, y_down, w_ref)
    send_weight(mp, core_other, w_ref)
    for j in (0, 1):
        count_copy(j).start()
    for i in (0, 1):
        fetches[1 + i].wait()
    for g in range(GROUPS):
        for i in (0, 1):
            for j in (0, 1):
                kv_copy(j, g, i).start()
    wfull[mp] = w_ref[...]

    ring_step(1, z_hi)
    await_weight(z_other)
    send_weight(z_other, y_up, wfull.at[z_other])
    send_weight(z_other, y_down, wfull.at[z_other])
    send_weight(z_other, core_other, wfull.at[z_other])
    for j in (0, 1):
        count_copy(j).wait_recv()
        count_copy(j + 2).start()
    ring_step(2, z_hi)
    relay_kv(0)
    ring_step(1, 1 - z_hi)
    relay_kv(1)
    ring_step(3, z_hi)
    ring_step(2, 1 - z_hi)
    relay_kv(2)
    ring_step(4, z_hi)
    ring_step(3, 1 - z_hi)
    relay_kv(3)
    ring_step(4, 1 - z_hi)

    for y_at in range(RING):
        for z_at in (0, 1):
            await_weight(slot_of(y_at, z_at, 1 - core))

    def weight_rows(g):
        per = SHARDS // GROUPS
        return wfull[g * per:(g + 1) * per].reshape(group_width, width)

    for fetch in fetches[3:]:
        fetch.wait()
    for g in range(GROUPS):
        grad[g] = dot(u_ref[...], weight_rows(g), CONTRACT_LAST).astype(jnp.bfloat16)

    for j in (2, 3):
        count_copy(j).wait_recv()

    positions = lax.broadcasted_iota(jnp.int32, (rows, 2 * rows), 0)
    first_half = lax.broadcasted_iota(jnp.int32, (rows, PAIR), 1) < HALF

    def stacked(pair):
        nothing = jnp.zeros_like(pair)
        return jnp.concatenate(
            [jnp.where(first_half, pair, nothing), jnp.where(first_half, nothing, pair)], axis=0
        )

    def heads_of(both):
        return jnp.concatenate([both[:HALF, :rows], both[HALF:, rows:]], axis=0)

    def part(value, e):
        return value[e * rows:(e + 1) * rows]

    def compute_pair(g, pp):
        columns = slice(pp * PAIR, (pp + 1) * PAIR)
        full = slice(g * group_width + pp * PAIR, g * group_width + (pp + 1) * PAIR)
        limits = [cnt_ref[0:1, :]]
        for j in range(4):
            limits.append(jnp.where(adj_ref[0, j] > 0, cr[j, 0:1, :], 0))
        queries = stacked(q_ref[:, full] * jnp.bfloat16(0.125))
        grad_pair = grad[g, :, columns]
        grads = stacked(grad_pair)
        keys = jnp.concatenate([k_ref[:, full]] + [kvr[j, g, 0, :, columns] for j in range(4)], axis=0)
        values = jnp.concatenate([v_ref[:, full]] + [kvr[j, g, 1, :, columns] for j in range(4)], axis=0)
        scores = dot(keys, queries, CONTRACT_LAST)
        masked = [jnp.where(positions < limits[e], part(scores, e), MASKED) for e in range(5)]
        largest = masked[0]
        for e in range(1, 5):
            largest = jnp.maximum(largest, masked[e])
        maxima = jnp.max(largest, axis=0, keepdims=True)
        expo = [jnp.exp(m - maxima) for m in masked]
        total = expo[0]
        for e in range(1, 5):
            total = total + expo[e]
        inverse = 1.0 / jnp.sum(total, axis=0, keepdims=True)
        probs = jnp.concatenate([m * inverse for m in expo], axis=0)
        rounded = probs.astype(jnp.bfloat16)
        attended = heads_of(dot(values, rounded, CONTRACT_FIRST)).astype(jnp.bfloat16).astype(jnp.float32)
        att[:, full] = attended.T.astype(jnp.bfloat16)
        product = attended * grad_pair.astype(jnp.float32).T
        delta = jnp.concatenate(
            [
                jnp.sum(product[:HALF], axis=0, keepdims=True),
                jnp.sum(product[HALF:], axis=0, keepdims=True),
            ],
            axis=1,
        )
        grad_scores = (probs * (dot(values, grads, CONTRACT_LAST) - delta)).astype(jnp.bfloat16)
        query_grad = heads_of(dot(keys, grad_scores, CONTRACT_FIRST)) * 0.125
        dq_ref[:, full] = query_grad.T.astype(jnp.bfloat16)
        key_terms = jnp.dot(grad_scores, queries, preferred_element_type=jnp.float32)
        value_terms = jnp.dot(rounded, grads, preferred_element_type=jnp.float32)
        for i, terms in ((0, key_terms), (1, value_terms)):
            own[g, i, :, columns] = part(terms, 0)
            for j in (0, 1):
                near[j, g, i, :, columns] = part(terms, j + 1)
                tsn[j + 2, g, i, :, columns] = part(terms, j + 3).astype(jnp.bfloat16)

    for g in range(GROUPS):
        for i in (0, 1):
            for j in (2, 3):
                kv_copy(j, g, i).wait_recv()
        for pp in range(group_width // PAIR):
            compute_pair(g, pp)
        for i in (0, 1):
            for j in (2, 3):
                term_copy(j, g, i).start()

    for g in range(GROUPS):
        for i in (0, 1):
            for j in (0, 1):
                term_copy(j + 2, g, i).wait_recv()
                tsn[j, g, i] = (near[j, g, i] + trc[j + 2, g, i].astype(jnp.float32)).astype(jnp.bfloat16)
                term_copy(j, g, i).start()

    whole = wfull[...].reshape(width, width)
    mix_ref[...] = jnp.dot(att[...], whole, preferred_element_type=jnp.float32).astype(jnp.bfloat16)

    for g in range(GROUPS):
        for i in (0, 1):
            total = own[g, i]
            for j in (0, 1):
                term_copy(j, g, i).wait_recv()
                total = total + trc[j, g, i].astype(jnp.float32)
            (dk_ref, dv_ref)[i][:, g * group_width:(g + 1) * group_width] = total.astype(jnp.bfloat16)

    for copy in w_copies:
        copy.wait_send()
    for j in range(4):
        count_copy(j).wait_send()
        for g in range(GROUPS):
            for i in (0, 1):
                kv_copy(j, g, i).wait_send()
                term_copy(j, g, i).wait_send()


def local(queries, keys, values, out_weight, upstream, adjacency, counts):
    rows, width = queries.shape
    group_width = width // GROUPS
    count_rows = jnp.broadcast_to(counts[:, None], (8, 2 * rows))
    hbm = pl.BlockSpec(memory_space=pltpu.HBM)
    vmem = pl.BlockSpec(memory_space=pltpu.VMEM)
    block = jax.ShapeDtypeStruct((rows, width), jnp.bfloat16)
    dma = pltpu.SemaphoreType.DMA
    pieces = (4, GROUPS, 2, rows, group_width)
    return pl.pallas_call(
        kernel,
        name="blocks",
        out_shape=(block, block, block, block),
        in_specs=[hbm] * 5 + [vmem] + [pl.BlockSpec(memory_space=pltpu.SMEM)],
        out_specs=(vmem, vmem, vmem, vmem),
        scratch_shapes=[
            pltpu.VMEM((rows, width), jnp.bfloat16),
            pltpu.VMEM((rows, width), jnp.bfloat16),
            pltpu.VMEM((rows, width), jnp.bfloat16),
            pltpu.VMEM((width // SHARDS, width), jnp.bfloat16),
            pltpu.VMEM((rows, width), jnp.bfloat16),
            dma((5,)),
            pltpu.VMEM((SHARDS, width // SHARDS, width), jnp.bfloat16),
            pltpu.VMEM(pieces, jnp.bfloat16),
            pltpu.VMEM((4, 8, 2 * rows), jnp.int32),
            pltpu.VMEM(pieces, jnp.bfloat16),
            pltpu.VMEM(pieces, jnp.bfloat16),
            pltpu.VMEM((2,) + pieces[1:], jnp.float32),
            pltpu.VMEM(pieces[1:], jnp.float32),
            pltpu.VMEM((rows, width), jnp.bfloat16),
            pltpu.VMEM((GROUPS, rows, group_width), jnp.bfloat16),
            dma((32,)),
            dma((SHARDS,)),
            dma((4, GROUPS, 2)),
            dma((4, GROUPS, 2)),
            dma((4,)),
            dma((4,)),
            dma((4, GROUPS, 2)),
            dma((4, GROUPS, 2)),
        ],
        compiler_params=pltpu.CompilerParams(
            collective_id=0, has_side_effects=True, vmem_limit_bytes=67_043_328
        ),
    )(queries, keys, values, out_weight, upstream, count_rows, adjacency)


def solution(mesh):
    both = P(("seq", "mp"), None)
    return jax.shard_map(
        local,
        mesh=mesh,
        in_specs=(both, both, both, P("mp", None), both, both, P(("seq", "mp"))),
        out_specs=(both, both, both, both),
        check_vma=False,
    )
```

```python
import jax
import jax.numpy as jnp
from jax import lax
from jax.experimental import pallas as pl
from jax.experimental.pallas import tpu as pltpu
from jax.sharding import PartitionSpec as P

GROUPS = 4
PAIR = 128
HALF = 64
SEQ = 16
SHARDS = 32
RING = 8
MASKED = -1e30
MESH = pl.DeviceIdType.MESH
CONTRACT_LAST = (((1,), (1,)), ((), ()))
CONTRACT_FIRST = (((0,), (0,)), ((), ()))


def dot(left, right, dims):
    return lax.dot_general(left, right, dims, preferred_element_type=jnp.float32)


def kernel(
    q_hbm, k_hbm, v_hbm, w_hbm, u_hbm, own_count, adj_ref,
    mix_hbm, dq_hbm, dk_hbm, dv_hbm,
    mix_ref, dq_ref, dk_ref, dv_ref, out_sem, cnt_ref,
    q_ref, k_ref, v_ref, w_ref, u_ref, in_sem, wfull, kvr, cr, tsn, trc, near, own, att, grad,
    w_send, w_recv, kv_send, kv_recv, c_send, c_recv, t_send, t_recv,
):
    seq = lax.axis_index("seq")
    mp = lax.axis_index("mp")
    rows, width = q_ref.shape
    group_width = width // GROUPS

    fetches = [
        pltpu.make_async_copy(source, target, in_sem.at[at])
        for at, (source, target) in enumerate(
            ((w_hbm, w_ref), (k_hbm, k_ref), (v_hbm, v_ref), (q_hbm, q_ref), (u_hbm, u_ref))
        )
    ]
    for fetch in fetches:
        fetch.start()
    cnt_ref[...] = jnp.full(cnt_ref.shape, own_count[0], jnp.int32)
    up = lax.rem(seq + 1, SEQ)
    down = lax.rem(seq + SEQ - 1, SEQ)
    y = mp // 4
    z_hi = lax.rem(mp // 2, 2)
    core = lax.rem(mp, 2)

    def slot_of(y_at, z_at, core_at):
        return y_at * 4 + z_at * 2 + core_at

    y_up = slot_of(lax.rem(y + 1, RING), z_hi, core)
    y_down = slot_of(lax.rem(y + RING - 1, RING), z_hi, core)
    z_other = slot_of(y, 1 - z_hi, core)
    mirror = (3 - seq // 4) * 4 + lax.rem(seq, 4)
    core_other = slot_of(y, z_hi, 1 - core)

    barrier = pltpu.get_barrier_semaphore()
    for target in (up, down):
        pl.semaphore_signal(barrier, inc=1, device_id=(target, mp), device_id_type=MESH)
    pl.semaphore_signal(barrier, inc=1, device_id=(mirror, z_other), device_id_type=MESH)
    for target in (y_up, y_down, core_other):
        pl.semaphore_signal(barrier, inc=1, device_id=(seq, target), device_id_type=MESH)
    pl.semaphore_wait(barrier, 6)

    w_copies = []

    def send_weight(slot, target, source, at=None):
        copy = pltpu.make_async_remote_copy(
            src_ref=source,
            dst_ref=wfull.at[slot],
            send_sem=w_send.at[len(w_copies)],
            recv_sem=w_recv.at[slot],
            device_id=(seq if at is None else at, target),
            device_id_type=MESH,
        )
        copy.start()
        w_copies.append(copy)

    def await_weight(slot):
        pltpu.make_async_remote_copy(
            src_ref=w_ref,
            dst_ref=wfull.at[slot],
            send_sem=w_send.at[0],
            recv_sem=w_recv.at[slot],
            device_id=(seq, core_other),
            device_id_type=MESH,
        ).wait_recv()

    def kv_copy(j, g, i):
        if j < 2:
            source = (k_ref, v_ref)[i].at[:, pl.ds(g * group_width, group_width)]
        else:
            source = kvr.at[j - 2, g, i]
        return pltpu.make_async_remote_copy(
            src_ref=source,
            dst_ref=kvr.at[j, g, i],
            send_sem=kv_send.at[j, g, i],
            recv_sem=kv_recv.at[j, g, i],
            device_id=((up, down)[j % 2], mp),
            device_id_type=MESH,
        )

    def count_copy(j):
        return pltpu.make_async_remote_copy(
            src_ref=cnt_ref if j < 2 else cr.at[j - 2],
            dst_ref=cr.at[j],
            send_sem=c_send.at[j],
            recv_sem=c_recv.at[j],
            device_id=((up, down)[j % 2], mp),
            device_id_type=MESH,
        )

    def term_copy(j, g, i):
        return pltpu.make_async_remote_copy(
            src_ref=tsn.at[j, g, i],
            dst_ref=trc.at[j, g, i],
            send_sem=t_send.at[j, g, i],
            recv_sem=t_recv.at[j, g, i],
            device_id=((down, up)[j % 2], mp),
            device_id_type=MESH,
        )

    def relay_kv(g):
        for i in (0, 1):
            for j in (0, 1):
                kv_copy(j, g, i).wait_recv()
                kv_copy(j + 2, g, i).start()

    def ring_step(step, z_at):
        slot = slot_of(lax.rem(y + RING - step, RING), z_at, core)
        await_weight(slot)
        if step < 4:
            send_weight(slot, y_up, wfull.at[slot])
        send_weight(slot, core_other, wfull.at[slot])
        if step < 4:
            slot = slot_of(lax.rem(y + step, RING), z_at, core)
            await_weight(slot)
            if step < 3:
                send_weight(slot, y_down, wfull.at[slot])
            send_weight(slot, core_other, wfull.at[slot])

    fetches[0].wait()
    send_weight(mp, z_other, w_ref, mirror)
    send_weight(mp, y_up, w_ref)
    send_weight(mp, y_down, w_ref)
    send_weight(mp, core_other, w_ref)
    for j in (0, 1):
        count_copy(j).start()
    for i in (0, 1):
        fetches[1 + i].wait()
    for g in range(GROUPS):
        for i in (0, 1):
            for j in (0, 1):
                kv_copy(j, g, i).start()
    wfull[mp] = w_ref[...]

    ring_step(1, z_hi)
    await_weight(z_other)
    send_weight(z_other, y_up, wfull.at[z_other])
    send_weight(z_other, y_down, wfull.at[z_other])
    send_weight(z_other, core_other, wfull.at[z_other])
    for j in (0, 1):
        count_copy(j).wait_recv()
        count_copy(j + 2).start()
    ring_step(2, z_hi)
    relay_kv(0)
    ring_step(1, 1 - z_hi)
    relay_kv(1)
    ring_step(3, z_hi)
    ring_step(2, 1 - z_hi)
    relay_kv(2)
    ring_step(4, z_hi)
    ring_step(3, 1 - z_hi)
    relay_kv(3)
    ring_step(4, 1 - z_hi)

    for y_at in range(RING):
        for z_at in (0, 1):
            await_weight(slot_of(y_at, z_at, 1 - core))

    def weight_rows(g):
        per = SHARDS // GROUPS
        return wfull[g * per:(g + 1) * per].reshape(group_width, width)

    for fetch in fetches[3:]:
        fetch.wait()
    for g in range(GROUPS):
        grad[g] = dot(u_ref[...], weight_rows(g), CONTRACT_LAST).astype(jnp.bfloat16)

    for j in (2, 3):
        count_copy(j).wait_recv()

    positions = lax.broadcasted_iota(jnp.int32, (rows, 2 * rows), 0)
    first_half = lax.broadcasted_iota(jnp.int32, (rows, PAIR), 1) < HALF

    def stacked(pair):
        nothing = jnp.zeros_like(pair)
        return jnp.concatenate(
            [jnp.where(first_half, pair, nothing), jnp.where(first_half, nothing, pair)], axis=0
        )

    def heads_of(both):
        return jnp.concatenate([both[:HALF, :rows], both[HALF:, rows:]], axis=0)

    def part(value, e):
        return value[e * rows:(e + 1) * rows]

    def compute_pair(g, pp):
        columns = slice(pp * PAIR, (pp + 1) * PAIR)
        full = slice(g * group_width + pp * PAIR, g * group_width + (pp + 1) * PAIR)
        limits = [cnt_ref[0:1, :]]
        for j in range(4):
            limits.append(jnp.where(adj_ref[0, j] > 0, cr[j, 0:1, :], 0))
        queries = stacked(q_ref[:, full] * jnp.bfloat16(0.125))
        grad_pair = grad[g, :, columns]
        grads = stacked(grad_pair)
        keys = jnp.concatenate([k_ref[:, full]] + [kvr[j, g, 0, :, columns] for j in range(4)], axis=0)
        values = jnp.concatenate([v_ref[:, full]] + [kvr[j, g, 1, :, columns] for j in range(4)], axis=0)
        scores = dot(keys, queries, CONTRACT_LAST)
        masked = [jnp.where(positions < limits[e], part(scores, e), MASKED) for e in range(5)]
        largest = masked[0]
        for e in range(1, 5):
            largest = jnp.maximum(largest, masked[e])
        maxima = jnp.max(largest, axis=0, keepdims=True)
        expo = [jnp.exp(m - maxima) for m in masked]
        total = expo[0]
        for e in range(1, 5):
            total = total + expo[e]
        inverse = 1.0 / jnp.sum(total, axis=0, keepdims=True)
        probs = jnp.concatenate([m * inverse for m in expo], axis=0)
        rounded = probs.astype(jnp.bfloat16)
        attended = heads_of(dot(values, rounded, CONTRACT_FIRST)).astype(jnp.bfloat16).astype(jnp.float32)
        att[:, full] = attended.T.astype(jnp.bfloat16)
        product = attended * grad_pair.astype(jnp.float32).T
        delta = jnp.concatenate(
            [
                jnp.sum(product[:HALF], axis=0, keepdims=True),
                jnp.sum(product[HALF:], axis=0, keepdims=True),
            ],
            axis=1,
        )
        grad_scores = (probs * (dot(values, grads, CONTRACT_LAST) - delta)).astype(jnp.bfloat16)
        query_grad = heads_of(dot(keys, grad_scores, CONTRACT_FIRST)) * 0.125
        dq_ref[:, full] = query_grad.T.astype(jnp.bfloat16)
        key_terms = jnp.dot(grad_scores, queries, preferred_element_type=jnp.float32)
        value_terms = jnp.dot(rounded, grads, preferred_element_type=jnp.float32)
        for i, terms in ((0, key_terms), (1, value_terms)):
            own[g, i, :, columns] = part(terms, 0)
            for j in (0, 1):
                near[j, g, i, :, columns] = part(terms, j + 1)
                tsn[j + 2, g, i, :, columns] = part(terms, j + 3).astype(jnp.bfloat16)

    for g in range(GROUPS):
        for i in (0, 1):
            for j in (2, 3):
                kv_copy(j, g, i).wait_recv()
        for pp in range(group_width // PAIR):
            compute_pair(g, pp)
        for i in (0, 1):
            for j in (2, 3):
                term_copy(j, g, i).start()

    for g in range(GROUPS):
        for i in (0, 1):
            for j in (0, 1):
                term_copy(j + 2, g, i).wait_recv()
                tsn[j, g, i] = (near[j, g, i] + trc[j + 2, g, i].astype(jnp.float32)).astype(jnp.bfloat16)
                term_copy(j, g, i).start()

    whole = wfull[...].reshape(width, width)
    query_copies = [
        pltpu.make_async_copy(dq_ref, dq_hbm, out_sem.at[0]),
        pltpu.make_async_copy(mix_ref, mix_hbm, out_sem.at[1]),
    ]
    query_copies[0].start()
    mix_ref[...] = jnp.dot(att[...], whole, preferred_element_type=jnp.float32).astype(jnp.bfloat16)

    def out_copy(g, i):
        columns = pl.ds(g * group_width, group_width)
        return pltpu.make_async_copy(
            (dk_ref, dv_ref)[i].at[g], (dk_hbm, dv_hbm)[i].at[:, columns], out_sem.at[2 + 2 * g + i]
        )

    for g in range(GROUPS):
        for i in (0, 1):
            total = own[g, i]
            for j in (0, 1):
                term_copy(j, g, i).wait_recv()
                total = total + trc[j, g, i].astype(jnp.float32)
            (dk_ref, dv_ref)[i][g] = total.astype(jnp.bfloat16)
        if g == 0:
            query_copies[1].start()
        for i in (0, 1):
            out_copy(g, i).start()

    for copy in query_copies:
        copy.wait()
    for g in range(GROUPS):
        for i in (0, 1):
            out_copy(g, i).wait()
    for copy in w_copies:
        copy.wait_send()
    for j in range(4):
        count_copy(j).wait_send()
        for g in range(GROUPS):
            for i in (0, 1):
                kv_copy(j, g, i).wait_send()
                term_copy(j, g, i).wait_send()


def place(*refs):
    sources, targets = refs[:4], refs[4:8]
    held, in_sem, out_sem = refs[8:]
    taken = [pltpu.make_async_copy(sources[n], held.at[n], in_sem.at[n]) for n in range(4)]
    given = [pltpu.make_async_copy(held.at[n], targets[n], out_sem.at[n]) for n in range(4)]
    for copy in taken:
        copy.start()
    for n in range(4):
        taken[n].wait()
        given[n].start()
    for copy in given:
        copy.wait()


def local(queries, keys, values, out_weight, upstream, adjacency, counts):
    rows, width = queries.shape
    group_width = width // GROUPS
    hbm = pl.BlockSpec(memory_space=pltpu.HBM)
    smem = pl.BlockSpec(memory_space=pltpu.SMEM)
    block = jax.ShapeDtypeStruct((rows, width), jnp.bfloat16)
    dma = pltpu.SemaphoreType.DMA
    pieces = (4, GROUPS, 2, rows, group_width)
    results = pl.pallas_call(
        kernel,
        name="blocks",
        out_shape=(block, block, block, block),
        in_specs=[hbm] * 5 + [smem] * 2,
        out_specs=(hbm, hbm, hbm, hbm),
        scratch_shapes=[
            pltpu.VMEM((rows, width), jnp.bfloat16),
            pltpu.VMEM((rows, width), jnp.bfloat16),
            pltpu.VMEM((GROUPS, rows, group_width), jnp.bfloat16),
            pltpu.VMEM((GROUPS, rows, group_width), jnp.bfloat16),
            dma((2 + 2 * GROUPS,)),
            pltpu.VMEM((8, 2 * rows), jnp.int32),
            pltpu.VMEM((rows, width), jnp.bfloat16),
            pltpu.VMEM((rows, width), jnp.bfloat16),
            pltpu.VMEM((rows, width), jnp.bfloat16),
            pltpu.VMEM((width // SHARDS, width), jnp.bfloat16),
            pltpu.VMEM((rows, width), jnp.bfloat16),
            dma((5,)),
            pltpu.VMEM((SHARDS, width // SHARDS, width), jnp.bfloat16),
            pltpu.VMEM(pieces, jnp.bfloat16),
            pltpu.VMEM((4, 8, 2 * rows), jnp.int32),
            pltpu.VMEM(pieces, jnp.bfloat16),
            pltpu.VMEM(pieces, jnp.bfloat16),
            pltpu.VMEM((2,) + pieces[1:], jnp.float32),
            pltpu.VMEM(pieces[1:], jnp.float32),
            pltpu.VMEM((rows, width), jnp.bfloat16),
            pltpu.VMEM((GROUPS, rows, group_width), jnp.bfloat16),
            dma((32,)),
            dma((SHARDS,)),
            dma((4, GROUPS, 2)),
            dma((4, GROUPS, 2)),
            dma((4,)),
            dma((4,)),
            dma((4, GROUPS, 2)),
            dma((4, GROUPS, 2)),
        ],
        compiler_params=pltpu.CompilerParams(
            collective_id=0, has_side_effects=True, vmem_limit_bytes=67_043_328
        ),
    )(queries, keys, values, out_weight, upstream, counts, adjacency)
    return pl.pallas_call(
        place,
        name="place",
        out_shape=(block, block, block, block),
        in_specs=[hbm] * 4,
        out_specs=(hbm, hbm, hbm, hbm),
        scratch_shapes=[pltpu.VMEM((4, rows, width), jnp.bfloat16), dma((4,)), dma((4,))],
        compiler_params=pltpu.CompilerParams(vmem_limit_bytes=67_043_328),
    )(*results)


def solution(mesh):
    both = P(("seq", "mp"), None)
    return jax.shard_map(
        local,
        mesh=mesh,
        in_specs=(both, both, both, P("mp", None), both, both, P(("seq", "mp"))),
        out_specs=(both, both, both, both),
        check_vma=False,
    )
```

```python
import jax
import jax.numpy as jnp
from jax import lax
from jax.experimental import pallas as pl
from jax.experimental.pallas import tpu as pltpu
from jax.sharding import PartitionSpec as P

GROUPS = 4
PAIR = 128
HALF = 64
SEQ = 16
SHARDS = 32
RING = 8
MASKED = -1e30
MESH = pl.DeviceIdType.MESH
CONTRACT_LAST = (((1,), (1,)), ((), ()))
CONTRACT_FIRST = (((0,), (0,)), ((), ()))


def dot(left, right, dims):
    return lax.dot_general(left, right, dims, preferred_element_type=jnp.float32)


def kernel(
    q_hbm, k_hbm, v_hbm, w_hbm, u_hbm, own_count, adj_ref,
    mix_hbm, dq_hbm, dk_hbm, dv_hbm,
    mix_ref, dq_ref, dk_ref, dv_ref, out_sem, cnt_ref,
    q_ref, k_ref, v_ref, w_ref, u_ref, in_sem, wfull, kvr, cr, tsn, trc, near, own, att, grad,
    held, turned, w_send, w_recv, kv_send, kv_recv, c_send, c_recv, t_send, t_recv,
):
    seq = lax.axis_index("seq")
    mp = lax.axis_index("mp")
    rows, width = q_ref.shape
    group_width = width // GROUPS

    fetches = [
        pltpu.make_async_copy(source, target, in_sem.at[at])
        for at, (source, target) in enumerate(
            ((w_hbm, w_ref), (k_hbm, k_ref), (v_hbm, v_ref), (q_hbm, q_ref), (u_hbm, u_ref))
        )
    ]
    for fetch in fetches:
        fetch.start()
    cnt_ref[...] = jnp.full(cnt_ref.shape, own_count[0], jnp.int32)
    up = lax.rem(seq + 1, SEQ)
    down = lax.rem(seq + SEQ - 1, SEQ)
    y = mp // 4
    z_hi = lax.rem(mp // 2, 2)
    core = lax.rem(mp, 2)

    def slot_of(y_at, z_at, core_at):
        return y_at * 4 + z_at * 2 + core_at

    y_up = slot_of(lax.rem(y + 1, RING), z_hi, core)
    y_down = slot_of(lax.rem(y + RING - 1, RING), z_hi, core)
    z_other = slot_of(y, 1 - z_hi, core)
    mirror = (3 - seq // 4) * 4 + lax.rem(seq, 4)
    core_other = slot_of(y, z_hi, 1 - core)

    barrier = pltpu.get_barrier_semaphore()
    for target in (up, down):
        pl.semaphore_signal(barrier, inc=1, device_id=(target, mp), device_id_type=MESH)
    pl.semaphore_signal(barrier, inc=1, device_id=(mirror, z_other), device_id_type=MESH)
    for target in (y_up, y_down, core_other):
        pl.semaphore_signal(barrier, inc=1, device_id=(seq, target), device_id_type=MESH)
    pl.semaphore_wait(barrier, 6)

    w_copies = []

    def send_weight(slot, target, source, at=None):
        copy = pltpu.make_async_remote_copy(
            src_ref=source,
            dst_ref=wfull.at[slot],
            send_sem=w_send.at[len(w_copies)],
            recv_sem=w_recv.at[slot],
            device_id=(seq if at is None else at, target),
            device_id_type=MESH,
        )
        copy.start()
        w_copies.append(copy)

    def await_weight(slot):
        pltpu.make_async_remote_copy(
            src_ref=w_ref,
            dst_ref=wfull.at[slot],
            send_sem=w_send.at[0],
            recv_sem=w_recv.at[slot],
            device_id=(seq, core_other),
            device_id_type=MESH,
        ).wait_recv()

    def kv_copy(j, g, i):
        if j < 2:
            source = (k_ref, v_ref)[i].at[:, pl.ds(g * group_width, group_width)]
        else:
            source = kvr.at[j - 2, g, i]
        return pltpu.make_async_remote_copy(
            src_ref=source,
            dst_ref=kvr.at[j, g, i],
            send_sem=kv_send.at[j, g, i],
            recv_sem=kv_recv.at[j, g, i],
            device_id=((up, down)[j % 2], mp),
            device_id_type=MESH,
        )

    def count_copy(j):
        return pltpu.make_async_remote_copy(
            src_ref=cnt_ref if j < 2 else cr.at[j - 2],
            dst_ref=cr.at[j],
            send_sem=c_send.at[j],
            recv_sem=c_recv.at[j],
            device_id=((up, down)[j % 2], mp),
            device_id_type=MESH,
        )

    def term_copy(j, g, i):
        return pltpu.make_async_remote_copy(
            src_ref=tsn.at[j, g, i],
            dst_ref=trc.at[j, g, i],
            send_sem=t_send.at[j, g, i],
            recv_sem=t_recv.at[j, g, i],
            device_id=((down, up)[j % 2], mp),
            device_id_type=MESH,
        )

    def relay_kv(g):
        for i in (0, 1):
            for j in (0, 1):
                kv_copy(j, g, i).wait_recv()
                kv_copy(j + 2, g, i).start()

    def ring_step(step, z_at):
        slot = slot_of(lax.rem(y + RING - step, RING), z_at, core)
        await_weight(slot)
        if step < 4:
            send_weight(slot, y_up, wfull.at[slot])
        send_weight(slot, core_other, wfull.at[slot])
        if step < 4:
            slot = slot_of(lax.rem(y + step, RING), z_at, core)
            await_weight(slot)
            if step < 3:
                send_weight(slot, y_down, wfull.at[slot])
            send_weight(slot, core_other, wfull.at[slot])

    fetches[0].wait()
    send_weight(mp, z_other, w_ref, mirror)
    send_weight(mp, y_up, w_ref)
    send_weight(mp, y_down, w_ref)
    send_weight(mp, core_other, w_ref)
    for j in (0, 1):
        count_copy(j).start()
    for i in (0, 1):
        fetches[1 + i].wait()
    for g in range(GROUPS):
        for i in (0, 1):
            for j in (0, 1):
                kv_copy(j, g, i).start()
    wfull[mp] = w_ref[...]

    ring_step(1, z_hi)
    await_weight(z_other)
    send_weight(z_other, y_up, wfull.at[z_other])
    send_weight(z_other, y_down, wfull.at[z_other])
    send_weight(z_other, core_other, wfull.at[z_other])
    for j in (0, 1):
        count_copy(j).wait_recv()
        count_copy(j + 2).start()
    ring_step(2, z_hi)
    relay_kv(0)
    ring_step(1, 1 - z_hi)
    relay_kv(1)
    ring_step(3, z_hi)
    ring_step(2, 1 - z_hi)
    relay_kv(2)
    ring_step(4, z_hi)
    ring_step(3, 1 - z_hi)
    relay_kv(3)
    ring_step(4, 1 - z_hi)

    def weight_rows(g):
        per = SHARDS // GROUPS
        return wfull[g * per:(g + 1) * per].reshape(group_width, width)

    for fetch in fetches[3:]:
        fetch.wait()
    for j in (2, 3):
        count_copy(j).wait_recv()

    positions = lax.broadcasted_iota(jnp.int32, (rows, 2 * rows), 0)
    first_half = lax.broadcasted_iota(jnp.int32, (rows, PAIR), 1) < HALF

    def stacked(pair):
        nothing = jnp.zeros_like(pair)
        return jnp.concatenate(
            [jnp.where(first_half, pair, nothing), jnp.where(first_half, nothing, pair)], axis=0
        )

    def heads_of(both):
        return jnp.concatenate([both[:HALF, :rows], both[HALF:, rows:]], axis=0)

    def part(value, e):
        return value[e * rows:(e + 1) * rows]

    def forward_pair(g, pp):
        columns = slice(pp * PAIR, (pp + 1) * PAIR)
        full = slice(g * group_width + pp * PAIR, g * group_width + (pp + 1) * PAIR)
        limits = [cnt_ref[0:1, :]]
        for j in range(4):
            limits.append(jnp.where(adj_ref[0, j] > 0, cr[j, 0:1, :], 0))
        queries = stacked(q_ref[:, full] * jnp.bfloat16(0.125))
        keys = jnp.concatenate([k_ref[:, full]] + [kvr[j, g, 0, :, columns] for j in range(4)], axis=0)
        values = jnp.concatenate([v_ref[:, full]] + [kvr[j, g, 1, :, columns] for j in range(4)], axis=0)
        scores = dot(keys, queries, CONTRACT_LAST)
        masked = [jnp.where(positions < limits[e], part(scores, e), MASKED) for e in range(5)]
        largest = masked[0]
        for e in range(1, 5):
            largest = jnp.maximum(largest, masked[e])
        maxima = jnp.max(largest, axis=0, keepdims=True)
        expo = [jnp.exp(m - maxima) for m in masked]
        total = expo[0]
        for e in range(1, 5):
            total = total + expo[e]
        inverse = 1.0 / jnp.sum(total, axis=0, keepdims=True)
        probs = jnp.concatenate([m * inverse for m in expo], axis=0)
        at = g * (group_width // PAIR) + pp
        held[at] = probs
        attended = heads_of(dot(values, probs.astype(jnp.bfloat16), CONTRACT_FIRST))
        attended = attended.astype(jnp.bfloat16).astype(jnp.float32)
        turned[at] = attended
        att[:, full] = attended.T.astype(jnp.bfloat16)

    def backward_pair(g, pp):
        columns = slice(pp * PAIR, (pp + 1) * PAIR)
        full = slice(g * group_width + pp * PAIR, g * group_width + (pp + 1) * PAIR)
        at = g * (group_width // PAIR) + pp
        queries = stacked(q_ref[:, full] * jnp.bfloat16(0.125))
        grad_pair = grad[g, :, columns]
        grads = stacked(grad_pair)
        keys = jnp.concatenate([k_ref[:, full]] + [kvr[j, g, 0, :, columns] for j in range(4)], axis=0)
        values = jnp.concatenate([v_ref[:, full]] + [kvr[j, g, 1, :, columns] for j in range(4)], axis=0)
        probs = held[at]
        rounded = probs.astype(jnp.bfloat16)
        attended = turned[at]
        product = attended * grad_pair.astype(jnp.float32).T
        delta = jnp.concatenate(
            [
                jnp.sum(product[:HALF], axis=0, keepdims=True),
                jnp.sum(product[HALF:], axis=0, keepdims=True),
            ],
            axis=1,
        )
        grad_scores = (probs * (dot(values, grads, CONTRACT_LAST) - delta)).astype(jnp.bfloat16)
        query_grad = heads_of(dot(keys, grad_scores, CONTRACT_FIRST)) * 0.125
        dq_ref[:, full] = query_grad.T.astype(jnp.bfloat16)
        key_terms = jnp.dot(grad_scores, queries, preferred_element_type=jnp.float32)
        value_terms = jnp.dot(rounded, grads, preferred_element_type=jnp.float32)
        for i, terms in ((0, key_terms), (1, value_terms)):
            own[g, i, :, columns] = part(terms, 0)
            for j in (0, 1):
                near[j, g, i, :, columns] = part(terms, j + 1)
                tsn[j + 2, g, i, :, columns] = part(terms, j + 3).astype(jnp.bfloat16)

    pairs = range(group_width // PAIR)

    def forward(g):
        for i in (0, 1):
            for j in (2, 3):
                kv_copy(j, g, i).wait_recv()
        for pp in pairs:
            forward_pair(g, pp)

    def backward(g):
        grad[g] = dot(u_ref[...], weight_rows(g), CONTRACT_LAST).astype(jnp.bfloat16)
        for pp in pairs:
            backward_pair(g, pp)
        for i in (0, 1):
            for j in (2, 3):
                term_copy(j, g, i).start()

    forward(0)
    for y_at in range(RING):
        for z_at in (0, 1):
            await_weight(slot_of(y_at, z_at, 1 - core))

    backward(0)
    for g in range(1, GROUPS):
        forward(g)
        backward(g)

    for g in range(GROUPS):
        for i in (0, 1):
            for j in (0, 1):
                term_copy(j + 2, g, i).wait_recv()
                tsn[j, g, i] = (near[j, g, i] + trc[j + 2, g, i].astype(jnp.float32)).astype(jnp.bfloat16)
                term_copy(j, g, i).start()

    whole = wfull[...].reshape(width, width)
    query_copies = [
        pltpu.make_async_copy(dq_ref, dq_hbm, out_sem.at[0]),
        pltpu.make_async_copy(mix_ref, mix_hbm, out_sem.at[1]),
    ]
    query_copies[0].start()
    mix_ref[...] = jnp.dot(att[...], whole, preferred_element_type=jnp.float32).astype(jnp.bfloat16)

    def out_copy(g, i):
        columns = pl.ds(g * group_width, group_width)
        return pltpu.make_async_copy(
            (dk_ref, dv_ref)[i].at[g], (dk_hbm, dv_hbm)[i].at[:, columns], out_sem.at[2 + 2 * g + i]
        )

    for g in range(GROUPS):
        for i in (0, 1):
            total = own[g, i]
            for j in (0, 1):
                term_copy(j, g, i).wait_recv()
                total = total + trc[j, g, i].astype(jnp.float32)
            (dk_ref, dv_ref)[i][g] = total.astype(jnp.bfloat16)
        if g == 0:
            query_copies[1].start()
        for i in (0, 1):
            out_copy(g, i).start()

    for copy in query_copies:
        copy.wait()
    for g in range(GROUPS):
        for i in (0, 1):
            out_copy(g, i).wait()
    for copy in w_copies:
        copy.wait_send()
    for j in range(4):
        count_copy(j).wait_send()
        for g in range(GROUPS):
            for i in (0, 1):
                kv_copy(j, g, i).wait_send()
                term_copy(j, g, i).wait_send()


def place(*refs):
    sources, targets = refs[:4], refs[4:8]
    held, in_sem, out_sem = refs[8:]
    taken = [pltpu.make_async_copy(sources[n], held.at[n], in_sem.at[n]) for n in range(4)]
    given = [pltpu.make_async_copy(held.at[n], targets[n], out_sem.at[n]) for n in range(4)]
    for copy in taken:
        copy.start()
    for n in range(4):
        taken[n].wait()
        given[n].start()
    for copy in given:
        copy.wait()


def local(queries, keys, values, out_weight, upstream, adjacency, counts):
    rows, width = queries.shape
    group_width = width // GROUPS
    hbm = pl.BlockSpec(memory_space=pltpu.HBM)
    smem = pl.BlockSpec(memory_space=pltpu.SMEM)
    block = jax.ShapeDtypeStruct((rows, width), jnp.bfloat16)
    dma = pltpu.SemaphoreType.DMA
    pieces = (4, GROUPS, 2, rows, group_width)
    results = pl.pallas_call(
        kernel,
        name="blocks",
        out_shape=(block, block, block, block),
        in_specs=[hbm] * 5 + [smem] * 2,
        out_specs=(hbm, hbm, hbm, hbm),
        scratch_shapes=[
            pltpu.VMEM((rows, width), jnp.bfloat16),
            pltpu.VMEM((rows, width), jnp.bfloat16),
            pltpu.VMEM((GROUPS, rows, group_width), jnp.bfloat16),
            pltpu.VMEM((GROUPS, rows, group_width), jnp.bfloat16),
            dma((2 + 2 * GROUPS,)),
            pltpu.VMEM((8, 2 * rows), jnp.int32),
            pltpu.VMEM((rows, width), jnp.bfloat16),
            pltpu.VMEM((rows, width), jnp.bfloat16),
            pltpu.VMEM((rows, width), jnp.bfloat16),
            pltpu.VMEM((width // SHARDS, width), jnp.bfloat16),
            pltpu.VMEM((rows, width), jnp.bfloat16),
            dma((5,)),
            pltpu.VMEM((SHARDS, width // SHARDS, width), jnp.bfloat16),
            pltpu.VMEM(pieces, jnp.bfloat16),
            pltpu.VMEM((4, 8, 2 * rows), jnp.int32),
            pltpu.VMEM(pieces, jnp.bfloat16),
            pltpu.VMEM(pieces, jnp.bfloat16),
            pltpu.VMEM((2,) + pieces[1:], jnp.float32),
            pltpu.VMEM(pieces[1:], jnp.float32),
            pltpu.VMEM((rows, width), jnp.bfloat16),
            pltpu.VMEM((GROUPS, rows, group_width), jnp.bfloat16),
            pltpu.VMEM((width // PAIR, 5 * rows, 2 * rows), jnp.float32),
            pltpu.VMEM((width // PAIR, PAIR, rows), jnp.float32),
            dma((32,)),
            dma((SHARDS,)),
            dma((4, GROUPS, 2)),
            dma((4, GROUPS, 2)),
            dma((4,)),
            dma((4,)),
            dma((4, GROUPS, 2)),
            dma((4, GROUPS, 2)),
        ],
        compiler_params=pltpu.CompilerParams(
            collective_id=0, has_side_effects=True, vmem_limit_bytes=67_043_328
        ),
    )(queries, keys, values, out_weight, upstream, counts, adjacency)
    return pl.pallas_call(
        place,
        name="place",
        out_shape=(block, block, block, block),
        in_specs=[hbm] * 4,
        out_specs=(hbm, hbm, hbm, hbm),
        scratch_shapes=[pltpu.VMEM((4, rows, width), jnp.bfloat16), dma((4,)), dma((4,))],
        compiler_params=pltpu.CompilerParams(vmem_limit_bytes=67_043_328),
    )(*results)


def solution(mesh):
    both = P(("seq", "mp"), None)
    return jax.shard_map(
        local,
        mesh=mesh,
        in_specs=(both, both, both, P("mp", None), both, both, P(("seq", "mp"))),
        out_specs=(both, both, both, both),
        check_vma=False,
    )
```

```python
import jax
import jax.numpy as jnp
from jax import lax
from jax.experimental import pallas as pl
from jax.experimental.pallas import tpu as pltpu
from jax.sharding import PartitionSpec as P

GROUPS = 8
PAIR = 128
HALF = 64
SEQ = 16
SHARDS = 32
RING = 8
MASKED = -1e30
MESH = pl.DeviceIdType.MESH
CONTRACT_LAST = (((1,), (1,)), ((), ()))
CONTRACT_FIRST = (((0,), (0,)), ((), ()))


def dot(left, right, dims):
    return lax.dot_general(left, right, dims, preferred_element_type=jnp.float32)


def kernel(
    q_hbm, k_hbm, v_hbm, w_hbm, u_hbm, own_count, adj_ref,
    mix_hbm, dq_hbm, dk_hbm, dv_hbm,
    mix_ref, dq_ref, dk_ref, dv_ref, out_sem, cnt_ref,
    q_ref, k_ref, v_ref, w_ref, u_ref, in_sem, wfull, kvr, cr, tsn, trc, near, own, att, grad,
    held, turned, w_send, w_recv, kv_send, kv_recv, c_send, c_recv, t_send, t_recv,
):
    seq = lax.axis_index("seq")
    mp = lax.axis_index("mp")
    rows, width = q_ref.shape
    group_width = width // GROUPS

    fetches = [
        pltpu.make_async_copy(source, target, in_sem.at[at])
        for at, (source, target) in enumerate(
            ((w_hbm, w_ref), (k_hbm, k_ref), (v_hbm, v_ref), (q_hbm, q_ref), (u_hbm, u_ref))
        )
    ]
    for fetch in fetches:
        fetch.start()
    cnt_ref[...] = jnp.full(cnt_ref.shape, own_count[0], jnp.int32)
    up = lax.rem(seq + 1, SEQ)
    down = lax.rem(seq + SEQ - 1, SEQ)
    y = mp // 4
    z_hi = lax.rem(mp // 2, 2)
    core = lax.rem(mp, 2)

    def slot_of(y_at, z_at, core_at):
        return y_at * 4 + z_at * 2 + core_at

    y_up = slot_of(lax.rem(y + 1, RING), z_hi, core)
    y_down = slot_of(lax.rem(y + RING - 1, RING), z_hi, core)
    z_other = slot_of(y, 1 - z_hi, core)
    mirror = (3 - seq // 4) * 4 + lax.rem(seq, 4)
    core_other = slot_of(y, z_hi, 1 - core)

    barrier = pltpu.get_barrier_semaphore()
    for target in (up, down):
        pl.semaphore_signal(barrier, inc=1, device_id=(target, mp), device_id_type=MESH)
    pl.semaphore_signal(barrier, inc=1, device_id=(mirror, z_other), device_id_type=MESH)
    for target in (y_up, y_down, core_other):
        pl.semaphore_signal(barrier, inc=1, device_id=(seq, target), device_id_type=MESH)
    pl.semaphore_wait(barrier, 6)

    w_copies = []

    def send_weight(slot, target, source, at=None):
        copy = pltpu.make_async_remote_copy(
            src_ref=source,
            dst_ref=wfull.at[slot],
            send_sem=w_send.at[len(w_copies)],
            recv_sem=w_recv.at[slot],
            device_id=(seq if at is None else at, target),
            device_id_type=MESH,
        )
        copy.start()
        w_copies.append(copy)

    def await_weight(slot):
        pltpu.make_async_remote_copy(
            src_ref=w_ref,
            dst_ref=wfull.at[slot],
            send_sem=w_send.at[0],
            recv_sem=w_recv.at[slot],
            device_id=(seq, core_other),
            device_id_type=MESH,
        ).wait_recv()

    def kv_copy(j, g, i):
        if j < 2:
            source = (k_ref, v_ref)[i].at[:, pl.ds(g * group_width, group_width)]
        else:
            source = kvr.at[j - 2, g, i]
        return pltpu.make_async_remote_copy(
            src_ref=source,
            dst_ref=kvr.at[j, g, i],
            send_sem=kv_send.at[j, g, i],
            recv_sem=kv_recv.at[j, g, i],
            device_id=((up, down)[j % 2], mp),
            device_id_type=MESH,
        )

    def count_copy(j):
        return pltpu.make_async_remote_copy(
            src_ref=cnt_ref if j < 2 else cr.at[j - 2],
            dst_ref=cr.at[j],
            send_sem=c_send.at[j],
            recv_sem=c_recv.at[j],
            device_id=((up, down)[j % 2], mp),
            device_id_type=MESH,
        )

    def term_copy(j, g, i):
        return pltpu.make_async_remote_copy(
            src_ref=tsn.at[j, g, i],
            dst_ref=trc.at[j, g, i],
            send_sem=t_send.at[j, g, i],
            recv_sem=t_recv.at[j, g, i],
            device_id=((down, up)[j % 2], mp),
            device_id_type=MESH,
        )

    def relay_kv(g):
        for i in (0, 1):
            for j in (0, 1):
                kv_copy(j, g, i).wait_recv()
                kv_copy(j + 2, g, i).start()

    def ring_step(step, z_at):
        slot = slot_of(lax.rem(y + RING - step, RING), z_at, core)
        await_weight(slot)
        if step < 4:
            send_weight(slot, y_up, wfull.at[slot])
        send_weight(slot, core_other, wfull.at[slot])
        if step < 4:
            slot = slot_of(lax.rem(y + step, RING), z_at, core)
            await_weight(slot)
            if step < 3:
                send_weight(slot, y_down, wfull.at[slot])
            send_weight(slot, core_other, wfull.at[slot])

    fetches[0].wait()
    send_weight(mp, z_other, w_ref, mirror)
    send_weight(mp, y_up, w_ref)
    send_weight(mp, y_down, w_ref)
    send_weight(mp, core_other, w_ref)
    for j in (0, 1):
        count_copy(j).start()
    for i in (0, 1):
        fetches[1 + i].wait()
    for g in range(GROUPS):
        for i in (0, 1):
            for j in (0, 1):
                kv_copy(j, g, i).start()
    wfull[mp] = w_ref[...]

    ring_step(1, z_hi)
    await_weight(z_other)
    send_weight(z_other, y_up, wfull.at[z_other])
    send_weight(z_other, y_down, wfull.at[z_other])
    send_weight(z_other, core_other, wfull.at[z_other])
    for j in (0, 1):
        count_copy(j).wait_recv()
        count_copy(j + 2).start()
    ring_step(2, z_hi)
    relay_kv(2 * 0)
    relay_kv(2 * 0 + 1)
    ring_step(1, 1 - z_hi)
    relay_kv(2 * 1)
    relay_kv(2 * 1 + 1)
    ring_step(3, z_hi)
    ring_step(2, 1 - z_hi)
    relay_kv(2 * 2)
    relay_kv(2 * 2 + 1)
    ring_step(4, z_hi)
    ring_step(3, 1 - z_hi)
    relay_kv(2 * 3)
    relay_kv(2 * 3 + 1)
    ring_step(4, 1 - z_hi)

    def weight_rows(g):
        per = SHARDS // GROUPS
        return wfull[g * per:(g + 1) * per].reshape(group_width, width)

    for fetch in fetches[3:]:
        fetch.wait()
    for j in (2, 3):
        count_copy(j).wait_recv()

    positions = lax.broadcasted_iota(jnp.int32, (rows, 2 * rows), 0)
    first_half = lax.broadcasted_iota(jnp.int32, (rows, PAIR), 1) < HALF

    def stacked(pair):
        nothing = jnp.zeros_like(pair)
        return jnp.concatenate(
            [jnp.where(first_half, pair, nothing), jnp.where(first_half, nothing, pair)], axis=0
        )

    def heads_of(both):
        return jnp.concatenate([both[:HALF, :rows], both[HALF:, rows:]], axis=0)

    def part(value, e):
        return value[e * rows:(e + 1) * rows]

    def forward_pair(g, pp):
        columns = slice(pp * PAIR, (pp + 1) * PAIR)
        full = slice(g * group_width + pp * PAIR, g * group_width + (pp + 1) * PAIR)
        limits = [cnt_ref[0:1, :]]
        for j in range(4):
            limits.append(jnp.where(adj_ref[0, j] > 0, cr[j, 0:1, :], 0))
        queries = stacked(q_ref[:, full] * jnp.bfloat16(0.125))
        keys = jnp.concatenate([k_ref[:, full]] + [kvr[j, g, 0, :, columns] for j in range(4)], axis=0)
        values = jnp.concatenate([v_ref[:, full]] + [kvr[j, g, 1, :, columns] for j in range(4)], axis=0)
        scores = dot(keys, queries, CONTRACT_LAST)
        masked = [jnp.where(positions < limits[e], part(scores, e), MASKED) for e in range(5)]
        largest = masked[0]
        for e in range(1, 5):
            largest = jnp.maximum(largest, masked[e])
        maxima = jnp.max(largest, axis=0, keepdims=True)
        expo = [jnp.exp(m - maxima) for m in masked]
        total = expo[0]
        for e in range(1, 5):
            total = total + expo[e]
        inverse = 1.0 / jnp.sum(total, axis=0, keepdims=True)
        probs = jnp.concatenate([m * inverse for m in expo], axis=0)
        at = g * (group_width // PAIR) + pp
        held[at] = probs
        attended = heads_of(dot(values, probs.astype(jnp.bfloat16), CONTRACT_FIRST))
        attended = attended.astype(jnp.bfloat16).astype(jnp.float32)
        turned[at] = attended
        att[:, full] = attended.T.astype(jnp.bfloat16)

    def backward_pair(g, pp):
        columns = slice(pp * PAIR, (pp + 1) * PAIR)
        full = slice(g * group_width + pp * PAIR, g * group_width + (pp + 1) * PAIR)
        at = g * (group_width // PAIR) + pp
        queries = stacked(q_ref[:, full] * jnp.bfloat16(0.125))
        grad_pair = grad[g, :, columns]
        grads = stacked(grad_pair)
        keys = jnp.concatenate([k_ref[:, full]] + [kvr[j, g, 0, :, columns] for j in range(4)], axis=0)
        values = jnp.concatenate([v_ref[:, full]] + [kvr[j, g, 1, :, columns] for j in range(4)], axis=0)
        probs = held[at]
        rounded = probs.astype(jnp.bfloat16)
        attended = turned[at]
        product = attended * grad_pair.astype(jnp.float32).T
        delta = jnp.concatenate(
            [
                jnp.sum(product[:HALF], axis=0, keepdims=True),
                jnp.sum(product[HALF:], axis=0, keepdims=True),
            ],
            axis=1,
        )
        grad_scores = (probs * (dot(values, grads, CONTRACT_LAST) - delta)).astype(jnp.bfloat16)
        query_grad = heads_of(dot(keys, grad_scores, CONTRACT_FIRST)) * 0.125
        dq_ref[:, full] = query_grad.T.astype(jnp.bfloat16)
        key_terms = jnp.dot(grad_scores, queries, preferred_element_type=jnp.float32)
        value_terms = jnp.dot(rounded, grads, preferred_element_type=jnp.float32)
        for i, terms in ((0, key_terms), (1, value_terms)):
            own[g, i, :, columns] = part(terms, 0)
            for j in (0, 1):
                near[j, g, i, :, columns] = part(terms, j + 1)
                tsn[j + 2, g, i, :, columns] = part(terms, j + 3).astype(jnp.bfloat16)

    pairs = range(group_width // PAIR)

    def forward(g):
        for i in (0, 1):
            for j in (2, 3):
                kv_copy(j, g, i).wait_recv()
        for pp in pairs:
            forward_pair(g, pp)

    def backward(g):
        grad[g] = dot(u_ref[...], weight_rows(g), CONTRACT_LAST).astype(jnp.bfloat16)
        for pp in pairs:
            backward_pair(g, pp)
        for i in (0, 1):
            for j in (2, 3):
                term_copy(j, g, i).start()

    forward(0)
    for y_at in range(RING):
        for z_at in (0, 1):
            await_weight(slot_of(y_at, z_at, 1 - core))

    backward(0)
    for g in range(1, GROUPS):
        forward(g)
        backward(g)

    for g in range(GROUPS):
        for i in (0, 1):
            for j in (0, 1):
                term_copy(j + 2, g, i).wait_recv()
                tsn[j, g, i] = (near[j, g, i] + trc[j + 2, g, i].astype(jnp.float32)).astype(jnp.bfloat16)
                term_copy(j, g, i).start()

    whole = wfull[...].reshape(width, width)
    query_copies = [
        pltpu.make_async_copy(dq_ref, dq_hbm, out_sem.at[0]),
        pltpu.make_async_copy(mix_ref, mix_hbm, out_sem.at[1]),
    ]
    query_copies[0].start()
    mix_ref[...] = jnp.dot(att[...], whole, preferred_element_type=jnp.float32).astype(jnp.bfloat16)

    def out_copy(g, i):
        columns = pl.ds(g * group_width, group_width)
        return pltpu.make_async_copy(
            (dk_ref, dv_ref)[i].at[g], (dk_hbm, dv_hbm)[i].at[:, columns], out_sem.at[2 + 2 * g + i]
        )

    for g in range(GROUPS):
        for i in (0, 1):
            total = own[g, i]
            for j in (0, 1):
                term_copy(j, g, i).wait_recv()
                total = total + trc[j, g, i].astype(jnp.float32)
            (dk_ref, dv_ref)[i][g] = total.astype(jnp.bfloat16)
        if g == 0:
            query_copies[1].start()
        for i in (0, 1):
            out_copy(g, i).start()

    for copy in query_copies:
        copy.wait()
    for g in range(GROUPS):
        for i in (0, 1):
            out_copy(g, i).wait()
    for copy in w_copies:
        copy.wait_send()
    for j in range(4):
        count_copy(j).wait_send()
        for g in range(GROUPS):
            for i in (0, 1):
                kv_copy(j, g, i).wait_send()
                term_copy(j, g, i).wait_send()


def place(*refs):
    sources, targets = refs[:4], refs[4:8]
    held, in_sem, out_sem = refs[8:]
    taken = [pltpu.make_async_copy(sources[n], held.at[n], in_sem.at[n]) for n in range(4)]
    given = [pltpu.make_async_copy(held.at[n], targets[n], out_sem.at[n]) for n in range(4)]
    for copy in taken:
        copy.start()
    for n in range(4):
        taken[n].wait()
        given[n].start()
    for copy in given:
        copy.wait()


def local(queries, keys, values, out_weight, upstream, adjacency, counts):
    rows, width = queries.shape
    group_width = width // GROUPS
    hbm = pl.BlockSpec(memory_space=pltpu.HBM)
    smem = pl.BlockSpec(memory_space=pltpu.SMEM)
    block = jax.ShapeDtypeStruct((rows, width), jnp.bfloat16)
    dma = pltpu.SemaphoreType.DMA
    pieces = (4, GROUPS, 2, rows, group_width)
    results = pl.pallas_call(
        kernel,
        name="blocks",
        out_shape=(block, block, block, block),
        in_specs=[hbm] * 5 + [smem] * 2,
        out_specs=(hbm, hbm, hbm, hbm),
        scratch_shapes=[
            pltpu.VMEM((rows, width), jnp.bfloat16),
            pltpu.VMEM((rows, width), jnp.bfloat16),
            pltpu.VMEM((GROUPS, rows, group_width), jnp.bfloat16),
            pltpu.VMEM((GROUPS, rows, group_width), jnp.bfloat16),
            dma((2 + 2 * GROUPS,)),
            pltpu.VMEM((8, 2 * rows), jnp.int32),
            pltpu.VMEM((rows, width), jnp.bfloat16),
            pltpu.VMEM((rows, width), jnp.bfloat16),
            pltpu.VMEM((rows, width), jnp.bfloat16),
            pltpu.VMEM((width // SHARDS, width), jnp.bfloat16),
            pltpu.VMEM((rows, width), jnp.bfloat16),
            dma((5,)),
            pltpu.VMEM((SHARDS, width // SHARDS, width), jnp.bfloat16),
            pltpu.VMEM(pieces, jnp.bfloat16),
            pltpu.VMEM((4, 8, 2 * rows), jnp.int32),
            pltpu.VMEM(pieces, jnp.bfloat16),
            pltpu.VMEM(pieces, jnp.bfloat16),
            pltpu.VMEM((2,) + pieces[1:], jnp.float32),
            pltpu.VMEM(pieces[1:], jnp.float32),
            pltpu.VMEM((rows, width), jnp.bfloat16),
            pltpu.VMEM((GROUPS, rows, group_width), jnp.bfloat16),
            pltpu.VMEM((width // PAIR, 5 * rows, 2 * rows), jnp.float32),
            pltpu.VMEM((width // PAIR, PAIR, rows), jnp.float32),
            dma((32,)),
            dma((SHARDS,)),
            dma((4, GROUPS, 2)),
            dma((4, GROUPS, 2)),
            dma((4,)),
            dma((4,)),
            dma((4, GROUPS, 2)),
            dma((4, GROUPS, 2)),
        ],
        compiler_params=pltpu.CompilerParams(
            collective_id=0, has_side_effects=True, vmem_limit_bytes=67_043_328
        ),
    )(queries, keys, values, out_weight, upstream, counts, adjacency)
    return pl.pallas_call(
        place,
        name="place",
        out_shape=(block, block, block, block),
        in_specs=[hbm] * 4,
        out_specs=(hbm, hbm, hbm, hbm),
        scratch_shapes=[pltpu.VMEM((4, rows, width), jnp.bfloat16), dma((4,)), dma((4,))],
        compiler_params=pltpu.CompilerParams(vmem_limit_bytes=67_043_328),
    )(*results)


def solution(mesh):
    both = P(("seq", "mp"), None)
    return jax.shard_map(
        local,
        mesh=mesh,
        in_specs=(both, both, both, P("mp", None), both, both, P(("seq", "mp"))),
        out_specs=(both, both, both, both),
        check_vma=False,
    )
```

```python
import jax
import jax.numpy as jnp
from jax import lax
from jax.experimental import pallas as pl
from jax.experimental.pallas import tpu as pltpu
from jax.sharding import PartitionSpec as P

GROUPS = 4
PAIR = 128
HALF = 64
SEQ = 16
SHARDS = 32
RING = 8
MASKED = -1e30
MESH = pl.DeviceIdType.MESH
CONTRACT_LAST = (((1,), (1,)), ((), ()))
CONTRACT_FIRST = (((0,), (0,)), ((), ()))


def dot(left, right, dims):
    return lax.dot_general(left, right, dims, preferred_element_type=jnp.float32)


def kernel(
    q_hbm, k_hbm, v_hbm, w_hbm, u_hbm, own_count, adj_ref,
    mix_hbm, dq_hbm, dk_hbm, dv_hbm,
    mix_ref, dq_ref, dk_ref, dv_ref, out_sem, cnt_ref,
    q_ref, k_ref, v_ref, w_ref, u_ref, in_sem, wfull, kvr, cr, tsn, trc, near, own, att, grad,
    held, turned, w_send, w_recv, kv_send, kv_recv, c_send, c_recv, t_send, t_recv,
):
    seq = lax.axis_index("seq")
    mp = lax.axis_index("mp")
    rows, width = q_ref.shape
    group_width = width // GROUPS

    fetches = [
        pltpu.make_async_copy(source, target, in_sem.at[at])
        for at, (source, target) in enumerate(
            ((w_hbm, w_ref), (k_hbm, k_ref), (v_hbm, v_ref), (q_hbm, q_ref), (u_hbm, u_ref))
        )
    ]
    for fetch in fetches:
        fetch.start()
    cnt_ref[...] = jnp.full(cnt_ref.shape, own_count[0], jnp.int32)
    up = lax.rem(seq + 1, SEQ)
    down = lax.rem(seq + SEQ - 1, SEQ)
    y = mp // 4
    z_hi = lax.rem(mp // 2, 2)
    core = lax.rem(mp, 2)

    def slot_of(y_at, z_at, core_at):
        return y_at * 4 + z_at * 2 + core_at

    y_up = slot_of(lax.rem(y + 1, RING), z_hi, core)
    y_down = slot_of(lax.rem(y + RING - 1, RING), z_hi, core)
    z_other = slot_of(y, 1 - z_hi, core)
    mirror = (3 - seq // 4) * 4 + lax.rem(seq, 4)
    core_other = slot_of(y, z_hi, 1 - core)

    barrier = pltpu.get_barrier_semaphore()
    for target in (up, down):
        pl.semaphore_signal(barrier, inc=1, device_id=(target, mp), device_id_type=MESH)
    pl.semaphore_signal(barrier, inc=1, device_id=(mirror, z_other), device_id_type=MESH)
    for target in (y_up, y_down, core_other):
        pl.semaphore_signal(barrier, inc=1, device_id=(seq, target), device_id_type=MESH)
    pl.semaphore_wait(barrier, 6)

    w_copies = []

    def send_weight(slot, target, source, at=None):
        copy = pltpu.make_async_remote_copy(
            src_ref=source,
            dst_ref=wfull.at[slot],
            send_sem=w_send.at[len(w_copies)],
            recv_sem=w_recv.at[slot],
            device_id=(seq if at is None else at, target),
            device_id_type=MESH,
        )
        copy.start()
        w_copies.append(copy)

    def await_weight(slot):
        pltpu.make_async_remote_copy(
            src_ref=w_ref,
            dst_ref=wfull.at[slot],
            send_sem=w_send.at[0],
            recv_sem=w_recv.at[slot],
            device_id=(seq, core_other),
            device_id_type=MESH,
        ).wait_recv()

    def kv_copy(j, g, i):
        if j < 2:
            source = (k_ref, v_ref)[i].at[:, pl.ds(g * group_width, group_width)]
        else:
            source = kvr.at[j - 2, g, i]
        return pltpu.make_async_remote_copy(
            src_ref=source,
            dst_ref=kvr.at[j, g, i],
            send_sem=kv_send.at[j, g, i],
            recv_sem=kv_recv.at[j, g, i],
            device_id=((up, down)[j % 2], mp),
            device_id_type=MESH,
        )

    def count_copy(j):
        return pltpu.make_async_remote_copy(
            src_ref=cnt_ref if j < 2 else cr.at[j - 2],
            dst_ref=cr.at[j],
            send_sem=c_send.at[j],
            recv_sem=c_recv.at[j],
            device_id=((up, down)[j % 2], mp),
            device_id_type=MESH,
        )

    def term_copy(j, g, i):
        return pltpu.make_async_remote_copy(
            src_ref=tsn.at[j, g, i],
            dst_ref=trc.at[j, g, i],
            send_sem=t_send.at[j, g, i],
            recv_sem=t_recv.at[j, g, i],
            device_id=((down, up)[j % 2], mp),
            device_id_type=MESH,
        )

    def relay_kv(g):
        for i in (0, 1):
            for j in (0, 1):
                kv_copy(j, g, i).wait_recv()
                kv_copy(j + 2, g, i).start()
        if g == 0:
            send_kv(GROUPS - 1)

    def send_kv(g):
        for i in (0, 1):
            for j in (0, 1):
                kv_copy(j, g, i).start()

    def ring_step(step, z_at):
        slot = slot_of(lax.rem(y + RING - step, RING), z_at, core)
        await_weight(slot)
        if step < 4:
            send_weight(slot, y_up, wfull.at[slot])
        send_weight(slot, core_other, wfull.at[slot])
        if step < 4:
            slot = slot_of(lax.rem(y + step, RING), z_at, core)
            await_weight(slot)
            if step < 3:
                send_weight(slot, y_down, wfull.at[slot])
            send_weight(slot, core_other, wfull.at[slot])

    fetches[0].wait()
    send_weight(mp, z_other, w_ref, mirror)
    send_weight(mp, y_up, w_ref)
    send_weight(mp, y_down, w_ref)
    send_weight(mp, core_other, w_ref)
    for j in (0, 1):
        count_copy(j).start()
    for i in (0, 1):
        fetches[1 + i].wait()
    for g in range(GROUPS - 1):
        send_kv(g)
    wfull[mp] = w_ref[...]

    ring_step(1, z_hi)
    await_weight(z_other)
    send_weight(z_other, y_up, wfull.at[z_other])
    send_weight(z_other, y_down, wfull.at[z_other])
    send_weight(z_other, core_other, wfull.at[z_other])
    for j in (0, 1):
        count_copy(j).wait_recv()
        count_copy(j + 2).start()
    relay_kv(0)
    ring_step(2, z_hi)
    ring_step(1, 1 - z_hi)
    relay_kv(1)
    ring_step(3, z_hi)
    ring_step(2, 1 - z_hi)
    relay_kv(2)
    ring_step(4, z_hi)
    ring_step(3, 1 - z_hi)
    relay_kv(3)
    ring_step(4, 1 - z_hi)

    def weight_rows(g):
        per = SHARDS // GROUPS
        return wfull[g * per:(g + 1) * per].reshape(group_width, width)

    for fetch in fetches[3:]:
        fetch.wait()
    for j in (2, 3):
        count_copy(j).wait_recv()

    positions = lax.broadcasted_iota(jnp.int32, (rows, 2 * rows), 0)
    first_half = lax.broadcasted_iota(jnp.int32, (rows, PAIR), 1) < HALF

    def stacked(pair):
        nothing = jnp.zeros_like(pair)
        return jnp.concatenate(
            [jnp.where(first_half, pair, nothing), jnp.where(first_half, nothing, pair)], axis=0
        )

    def heads_of(both):
        return jnp.concatenate([both[:HALF, :rows], both[HALF:, rows:]], axis=0)

    def part(value, e):
        return value[e * rows:(e + 1) * rows]

    def forward_pair(g, pp):
        columns = slice(pp * PAIR, (pp + 1) * PAIR)
        full = slice(g * group_width + pp * PAIR, g * group_width + (pp + 1) * PAIR)
        limits = [cnt_ref[0:1, :]]
        for j in range(4):
            limits.append(jnp.where(adj_ref[0, j] > 0, cr[j, 0:1, :], 0))
        queries = stacked(q_ref[:, full] * jnp.bfloat16(0.125))
        keys = jnp.concatenate([k_ref[:, full]] + [kvr[j, g, 0, :, columns] for j in range(4)], axis=0)
        values = jnp.concatenate([v_ref[:, full]] + [kvr[j, g, 1, :, columns] for j in range(4)], axis=0)
        scores = dot(keys, queries, CONTRACT_LAST)
        masked = [jnp.where(positions < limits[e], part(scores, e), MASKED) for e in range(5)]
        largest = masked[0]
        for e in range(1, 5):
            largest = jnp.maximum(largest, masked[e])
        maxima = jnp.max(largest, axis=0, keepdims=True)
        expo = [jnp.exp(m - maxima) for m in masked]
        total = expo[0]
        for e in range(1, 5):
            total = total + expo[e]
        inverse = 1.0 / jnp.sum(total, axis=0, keepdims=True)
        probs = jnp.concatenate([m * inverse for m in expo], axis=0)
        at = g * (group_width // PAIR) + pp
        held[at] = probs
        attended = heads_of(dot(values, probs.astype(jnp.bfloat16), CONTRACT_FIRST))
        attended = attended.astype(jnp.bfloat16).astype(jnp.float32)
        turned[at] = attended
        att[:, full] = attended.T.astype(jnp.bfloat16)

    def backward_pair(g, pp):
        columns = slice(pp * PAIR, (pp + 1) * PAIR)
        full = slice(g * group_width + pp * PAIR, g * group_width + (pp + 1) * PAIR)
        at = g * (group_width // PAIR) + pp
        queries = stacked(q_ref[:, full] * jnp.bfloat16(0.125))
        grad_pair = grad[g, :, columns]
        grads = stacked(grad_pair)
        keys = jnp.concatenate([k_ref[:, full]] + [kvr[j, g, 0, :, columns] for j in range(4)], axis=0)
        values = jnp.concatenate([v_ref[:, full]] + [kvr[j, g, 1, :, columns] for j in range(4)], axis=0)
        probs = held[at]
        rounded = probs.astype(jnp.bfloat16)
        attended = turned[at]
        product = attended * grad_pair.astype(jnp.float32).T
        delta = jnp.concatenate(
            [
                jnp.sum(product[:HALF], axis=0, keepdims=True),
                jnp.sum(product[HALF:], axis=0, keepdims=True),
            ],
            axis=1,
        )
        grad_scores = (probs * (dot(values, grads, CONTRACT_LAST) - delta)).astype(jnp.bfloat16)
        query_grad = heads_of(dot(keys, grad_scores, CONTRACT_FIRST)) * 0.125
        dq_ref[:, full] = query_grad.T.astype(jnp.bfloat16)
        key_terms = jnp.dot(grad_scores, queries, preferred_element_type=jnp.float32)
        value_terms = jnp.dot(rounded, grads, preferred_element_type=jnp.float32)
        for i, terms in ((0, key_terms), (1, value_terms)):
            own[g, i, :, columns] = part(terms, 0)
            for j in (0, 1):
                near[j, g, i, :, columns] = part(terms, j + 1)
                tsn[j + 2, g, i, :, columns] = part(terms, j + 3).astype(jnp.bfloat16)

    pairs = range(group_width // PAIR)

    def forward(g):
        for i in (0, 1):
            for j in (2, 3):
                kv_copy(j, g, i).wait_recv()
        for pp in pairs:
            forward_pair(g, pp)

    def backward(g):
        grad[g] = dot(u_ref[...], weight_rows(g), CONTRACT_LAST).astype(jnp.bfloat16)
        for pp in pairs:
            backward_pair(g, pp)
        for i in (0, 1):
            for j in (2, 3):
                term_copy(j, g, i).start()

    forward(0)
    for y_at in range(RING):
        for z_at in (0, 1):
            await_weight(slot_of(y_at, z_at, 1 - core))

    backward(0)
    for g in range(1, GROUPS):
        forward(g)
        backward(g)

    for g in range(GROUPS):
        for i in (0, 1):
            for j in (0, 1):
                term_copy(j + 2, g, i).wait_recv()
                tsn[j, g, i] = (near[j, g, i] + trc[j + 2, g, i].astype(jnp.float32)).astype(jnp.bfloat16)
                term_copy(j, g, i).start()

    whole = wfull[...].reshape(width, width)
    query_copies = [
        pltpu.make_async_copy(dq_ref, dq_hbm, out_sem.at[0]),
        pltpu.make_async_copy(mix_ref, mix_hbm, out_sem.at[1]),
    ]
    query_copies[0].start()
    mix_ref[...] = jnp.dot(att[...], whole, preferred_element_type=jnp.float32).astype(jnp.bfloat16)

    def out_copy(g, i):
        columns = pl.ds(g * group_width, group_width)
        return pltpu.make_async_copy(
            (dk_ref, dv_ref)[i].at[g], (dk_hbm, dv_hbm)[i].at[:, columns], out_sem.at[2 + 2 * g + i]
        )

    for g in range(GROUPS):
        for i in (0, 1):
            total = own[g, i]
            for j in (0, 1):
                term_copy(j, g, i).wait_recv()
                total = total + trc[j, g, i].astype(jnp.float32)
            (dk_ref, dv_ref)[i][g] = total.astype(jnp.bfloat16)
        if g == 0:
            query_copies[1].start()
        for i in (0, 1):
            out_copy(g, i).start()

    for copy in query_copies:
        copy.wait()
    for g in range(GROUPS):
        for i in (0, 1):
            out_copy(g, i).wait()
    for copy in w_copies:
        copy.wait_send()
    for j in range(4):
        count_copy(j).wait_send()
        for g in range(GROUPS):
            for i in (0, 1):
                kv_copy(j, g, i).wait_send()
                term_copy(j, g, i).wait_send()


def place(*refs):
    sources, targets = refs[:4], refs[4:8]
    held, in_sem, out_sem = refs[8:]
    taken = [pltpu.make_async_copy(sources[n], held.at[n], in_sem.at[n]) for n in range(4)]
    given = [pltpu.make_async_copy(held.at[n], targets[n], out_sem.at[n]) for n in range(4)]
    for copy in taken:
        copy.start()
    for n in range(4):
        taken[n].wait()
        given[n].start()
    for copy in given:
        copy.wait()


def local(queries, keys, values, out_weight, upstream, adjacency, counts):
    rows, width = queries.shape
    group_width = width // GROUPS
    hbm = pl.BlockSpec(memory_space=pltpu.HBM)
    smem = pl.BlockSpec(memory_space=pltpu.SMEM)
    block = jax.ShapeDtypeStruct((rows, width), jnp.bfloat16)
    dma = pltpu.SemaphoreType.DMA
    pieces = (4, GROUPS, 2, rows, group_width)
    results = pl.pallas_call(
        kernel,
        name="blocks",
        out_shape=(block, block, block, block),
        in_specs=[hbm] * 5 + [smem] * 2,
        out_specs=(hbm, hbm, hbm, hbm),
        scratch_shapes=[
            pltpu.VMEM((rows, width), jnp.bfloat16),
            pltpu.VMEM((rows, width), jnp.bfloat16),
            pltpu.VMEM((GROUPS, rows, group_width), jnp.bfloat16),
            pltpu.VMEM((GROUPS, rows, group_width), jnp.bfloat16),
            dma((2 + 2 * GROUPS,)),
            pltpu.VMEM((8, 2 * rows), jnp.int32),
            pltpu.VMEM((rows, width), jnp.bfloat16),
            pltpu.VMEM((rows, width), jnp.bfloat16),
            pltpu.VMEM((rows, width), jnp.bfloat16),
            pltpu.VMEM((width // SHARDS, width), jnp.bfloat16),
            pltpu.VMEM((rows, width), jnp.bfloat16),
            dma((5,)),
            pltpu.VMEM((SHARDS, width // SHARDS, width), jnp.bfloat16),
            pltpu.VMEM(pieces, jnp.bfloat16),
            pltpu.VMEM((4, 8, 2 * rows), jnp.int32),
            pltpu.VMEM(pieces, jnp.bfloat16),
            pltpu.VMEM(pieces, jnp.bfloat16),
            pltpu.VMEM((2,) + pieces[1:], jnp.float32),
            pltpu.VMEM(pieces[1:], jnp.float32),
            pltpu.VMEM((rows, width), jnp.bfloat16),
            pltpu.VMEM((GROUPS, rows, group_width), jnp.bfloat16),
            pltpu.VMEM((width // PAIR, 5 * rows, 2 * rows), jnp.float32),
            pltpu.VMEM((width // PAIR, PAIR, rows), jnp.float32),
            dma((32,)),
            dma((SHARDS,)),
            dma((4, GROUPS, 2)),
            dma((4, GROUPS, 2)),
            dma((4,)),
            dma((4,)),
            dma((4, GROUPS, 2)),
            dma((4, GROUPS, 2)),
        ],
        compiler_params=pltpu.CompilerParams(
            collective_id=0, has_side_effects=True, vmem_limit_bytes=67_043_328
        ),
    )(queries, keys, values, out_weight, upstream, counts, adjacency)
    return pl.pallas_call(
        place,
        name="place",
        out_shape=(block, block, block, block),
        in_specs=[hbm] * 4,
        out_specs=(hbm, hbm, hbm, hbm),
        scratch_shapes=[pltpu.VMEM((4, rows, width), jnp.bfloat16), dma((4,)), dma((4,))],
        compiler_params=pltpu.CompilerParams(vmem_limit_bytes=67_043_328),
    )(*results)


def solution(mesh):
    both = P(("seq", "mp"), None)
    return jax.shard_map(
        local,
        mesh=mesh,
        in_specs=(both, both, both, P("mp", None), both, both, P(("seq", "mp"))),
        out_specs=(both, both, both, both),
        check_vma=False,
    )
```
